32 devices in a mesh: dp: 16 (over z, x, core), expert: 2 (over y).
Axes of the slice: x: 2, y: 2, z: 4, core: 2. Of those that a mesh axis runs over, the one named last changes fastest.
Arguments:
- hidden: bfloat16 [1024, 8192], P(('dp', 'expert')), may hold values from -6 to 6
- out_grad: bfloat16 [1024, 6144], P(('dp', 'expert')), may hold values from -6 to 6
- counts: int32 [32, 2], P(('dp', 'expert')), may hold values from 0 to 20, as said below
- route_index: int32 [32, 32], P(('dp', 'expert')), may hold values from 0 to 31, each once within a row
- keep: int32 [16], replicated, may hold values 0 or 1
Outputs:
- grad_blocks: float32 [2, 16, 2048, 1536], P('expert', 'dp')
- block_scales: float32 [2, 16, 2048, 12], P('expert', 'dp')
The draws below stay inside these ranges and needn't reach their ends.
Inputs may be any that keep to these rules, and one draw needn't show every extreme that they name: Each row of counts sums to 32; for every index of dp, one expert receives exactly 20 rows from each of the 2 devices of that index.
All inputs are finite; a program needn't handle non-finite values. Where the reference program divides by a largest or mean magnitude, that divisor is 1e-20 or more.
Results may differ from the reference program's by a relative error of at most 0.0003.
Values may be sent and summed in bfloat16 or wider, within the bound.
A program may use at most 128 MiB of HBM per device.

```python
import jax
import jax.numpy as jnp
from jax import lax

D = 6144
HW = 8192
TOK_DEV = 32
CAP = 20
Q = 4
TOKENS = 1024
N_DP = 16
N_EXPERT = 2


def draw_counts(key, part):
    experts = N_EXPERT
    devices = N_DP * N_EXPERT
    key_hot = jax.random.fold_in(key, 11)
    key_weight = jax.random.fold_in(key, 23)
    hot = jax.random.randint(key_hot, (N_DP,), 0, experts)
    hot_dev = jnp.repeat(hot, experts)
    others = experts - 1
    rest = TOK_DEV - CAP
    weights = jax.random.randint(key_weight, (devices, others), 1, 3)
    total = jnp.sum(weights, axis=1, keepdims=True)
    base = rest * weights // total
    remain = rest - jnp.sum(base, axis=1, keepdims=True)
    extra = (jnp.arange(others)[None, :] < remain).astype(jnp.int32)
    split = base + extra
    column = jnp.arange(experts)[None, :]
    offset = (column - hot_dev[:, None] - 1) % experts
    offset = jnp.minimum(offset, others - 1)
    values = jnp.take_along_axis(split, offset, axis=1)
    result = jnp.where(column == hot_dev[:, None], CAP, values)
    return result.astype(jnp.int32)


def place_ends(array, stream_key, least, largest):
    index_at = [jax.random.randint(jax.random.fold_in(stream_key, axis), (), 0, length) for axis, length in enumerate(array.shape)]
    widest = array.shape.index(max(array.shape))
    beside = index_at[:widest] + [(index_at[widest] + 1) % array.shape[widest]] + index_at[widest + 1:]
    return array.at[tuple(index_at)].set(least).at[tuple(beside)].set(largest)


def block_levels(key, dims, shards, low, top_value):
    factor_of = 1.0
    for dim, blocks in shards:
        heights = jax.random.uniform(jax.random.fold_in(jax.random.fold_in(key, 6), dim), (blocks,), jnp.float32, low / len(shards), top_value / len(shards))
        factor_of = factor_of * jnp.repeat(jnp.exp(heights), dims[dim] // blocks).reshape((-1,) + (1,) * (len(dims) - 1 - dim))
    return factor_of


def normal_values(key, shape, width, limit, cuts=(), kind=jnp.bfloat16):
    array = width * jax.random.normal(key, shape, jnp.float32)
    if cuts:
        array = array * block_levels(key, shape, cuts, -0.22, 0.18)
    return jnp.clip(array, -limit, limit).astype(kind)


def setup_inputs(seed: int = 0) -> dict:
    arg_keys = jax.random.split(jax.random.key(seed), 6)
    return {
        "hidden": normal_values(arg_keys[0], (TOKENS, HW), 1.0, 6.0, ((0, 32),)),
        "out_grad": normal_values(arg_keys[1], (TOKENS, D), 1.0, 6.0, ((0, 32),)),
        "counts": draw_counts(jax.random.fold_in(arg_keys[5], 71), 0),
        "route_index": jax.vmap(lambda own: jax.random.permutation(own, TOK_DEV))(jax.random.split(arg_keys[3], (N_DP * N_EXPERT))).reshape((N_DP * N_EXPERT, TOK_DEV)).astype(jnp.int32),
        "keep": place_ends((jax.random.randint(arg_keys[4], (N_DP,), 0, 4) < 3).astype(jnp.int32), jax.random.fold_in(arg_keys[4], 1), 0, 1),
    }


def expert_rows(rows_dev, counts_dev, perm_dev, expert_id):
    offsets = jnp.cumsum(counts_dev) - counts_dev
    start = offsets[expert_id]
    count = counts_dev[expert_id]
    slots = jnp.arange(CAP, dtype=jnp.int32)
    position = jnp.minimum(start + slots, TOK_DEV - 1).astype(jnp.int32)
    local = perm_dev[position]
    picked = rows_dev[local]
    return jnp.where((slots < count)[:, None], picked, jnp.zeros_like(picked))


def reference(hidden, out_grad, counts, route_index, keep):
    ndev = N_DP * N_EXPERT
    hid_dev = hidden.reshape(ndev, TOK_DEV, HW)
    grad_dev = out_grad.reshape(ndev, TOK_DEV, D)
    keep_dev = jnp.repeat(keep, N_EXPERT)
    grad_dev = jnp.where((keep_dev > 0)[:, None, None], grad_dev, jnp.zeros_like(grad_dev))
    kept = jnp.sum(keep).astype(jnp.float32)
    factor = jnp.float32(N_DP) / jnp.maximum(kept, jnp.float32(1.0))
    tile_rows = HW // Q
    tile_cols = D // Q

    def one_expert(expert_id):
        gather_rows = jax.vmap(expert_rows, in_axes=(0, 0, 0, None))
        rows_h = gather_rows(hid_dev, counts, route_index, expert_id).reshape(ndev * CAP, HW)
        rows_g = gather_rows(grad_dev, counts, route_index, expert_id).reshape(ndev * CAP, D)
        grad = lax.dot_general(rows_h, rows_g, (((0,), (0,)), ((), ())), preferred_element_type=jnp.float32)
        grad = grad * factor
        blocked = grad.reshape(HW, D // 128, 128)
        scales = jnp.max(jnp.abs(blocked), axis=-1)
        normed = (blocked / (scales[..., None] + 1e-6)).reshape(HW, D)
        tiles = normed.reshape(Q, tile_rows, Q, tile_cols).transpose(0, 2, 1, 3).reshape(N_DP, tile_rows, tile_cols)
        scale_tiles = scales.reshape(Q, tile_rows, Q, tile_cols // 128).transpose(0, 2, 1, 3).reshape(N_DP, tile_rows, tile_cols // 128)
        return tiles, scale_tiles

    return lax.map(one_expert, jnp.arange(N_EXPERT, dtype=jnp.int32))
```

```python
import functools
import math

import jax
import jax.numpy as jnp
from jax import lax
from jax.experimental import pallas as pl
from jax.experimental.pallas import tpu as pltpu
from jax.sharding import PartitionSpec as P

MESH = pl.DeviceIdType.MESH
LANES = 128
SUB = 16


def swapped(block, axis, bit):
    count = lax.axis_size(axis)
    route = []
    for low in range(count):
        high = low | 1 << bit
        if high != low and high < count:
            route += [(low, high), (high, low)]
    return lax.ppermute(block, axis, route)


def build_slots(rows_dev, counts_dev, perm_dev, capacity):
    ids = jnp.arange(counts_dev.shape[0], dtype=jnp.int32)
    before = ids[None, :] < ids[:, None]
    offsets = jnp.sum(jnp.where(before, counts_dev[None, :], 0), axis=1)
    slots = jnp.arange(capacity, dtype=jnp.int32)
    position = offsets[:, None] + slots[None, :]
    position = jnp.minimum(position, rows_dev.shape[0] - 1)
    live = slots[None, :] < counts_dev[:, None]
    local = perm_dev[position]
    picked = rows_dev[local]
    return jnp.where(live[:, :, None], picked, jnp.zeros_like(picked))


def join_pair(mine, partner, replica, bit):
    lower = replica >> bit & 1 == 0
    first = jnp.concatenate([mine, partner], axis=1)
    second = jnp.concatenate([partner, mine], axis=1)
    return jnp.where(lower, first, second)


def gather_general(hidden, out_grad, counts, route_index, keep, capacity):
    experts = lax.axis_size("expert")
    replicas = lax.axis_size("dp")
    side = math.isqrt(replicas)
    levels = side.bit_length() - 1
    replica = lax.axis_index("dp")
    hidden_units = hidden.shape[1]
    width = out_grad.shape[1]
    grad_rows = jnp.where(keep[replica] > 0, out_grad, jnp.zeros_like(out_grad))
    send_h = build_slots(hidden, counts[0], route_index[0], capacity)
    send_g = build_slots(grad_rows, counts[0], route_index[0], capacity)
    recv_h = lax.all_to_all(send_h, "expert", split_axis=0, concat_axis=0, tiled=True)
    recv_g = lax.all_to_all(send_g, "expert", split_axis=0, concat_axis=0, tiled=True)
    slot_count = experts * capacity
    tile_rows = hidden_units // side
    tile_cols = width // side
    sub_rows = slot_count // side
    piece_h = (
        recv_h.reshape(side, sub_rows, side, tile_rows)
        .transpose(2, 0, 1, 3)
        .reshape(replicas, sub_rows, tile_rows)
    )
    piece_g = (
        recv_g.reshape(side, sub_rows, side, tile_cols)
        .transpose(0, 2, 1, 3)
        .reshape(replicas, sub_rows, tile_cols)
    )
    all_h = lax.all_to_all(piece_h, "dp", split_axis=0, concat_axis=0, tiled=True)
    all_g = lax.all_to_all(piece_g, "dp", split_axis=0, concat_axis=0, tiled=True)
    for bit in range(levels):
        all_h = join_pair(all_h, swapped(all_h, "dp", bit), replica, bit)
    for bit in range(levels, 2 * levels):
        all_g = join_pair(all_g, swapped(all_g, "dp", bit), replica, bit)
    return [(all_h.reshape(-1, tile_rows), all_g.reshape(-1, tile_cols))]


def spread_kernel(
    n, low, counts_in, keep_in, route_in, hidden_in, grad_in, h0, g0m, hb, gb, hx, gx,
    counts, keep, route, hidden, grad, g0, h0s, g0s, hbs, gbs, hys, gys, hyr, gyr,
    in_sem, send_sem, h_sem, g_sem, hx_sem, gx_sem, y_sem, own_sem,
):
    here = lax.axis_index("dp")
    y = lax.axis_index("expert")
    z, q = here // n, here % n
    twin = q + 1 - 2 * (q % 2)
    over = (q + n // 2) % n
    far = (twin + n // 2) % n
    zs = [(z + d) % n for d in range(n)]
    half = SUB // 2
    gcols = gb.shape[3]

    moves = []
    for src, dst in ((counts_in, counts), (keep_in, keep), (route_in, route)):
        moves.append(pltpu.make_async_copy(src, dst, in_sem.at[len(moves)]))
    for src, dst in ((grad_in, grad), (hidden_in, hidden)):
        cols = src.shape[1] // n
        for part in range(n):
            cut = (slice(None), pl.ds(part * cols, cols))
            moves.append(pltpu.make_async_copy(src.at[cut], dst.at[cut], in_sem.at[len(moves)]))
    for move in moves:
        move.start()

    barrier = pltpu.get_barrier_semaphore()
    peers = [(here, 1 - y)]
    peers += [(z * n + to, y) for to in (over, twin, far)]
    peers += [(zs[d] * n + q, y) for d in range(1, n)]
    for peer in peers:
        pl.semaphore_signal(barrier, inc=1, device_id=peer, device_id_type=MESH)

    for move in moves[:3]:
        move.wait()
    due = moves[3:]
    rows = hidden.shape[0]
    total = 3 * SUB
    row = lax.broadcasted_iota(jnp.int32, (total, rows), 0)
    pos = lax.broadcasted_iota(jnp.int32, (total, rows), 1)
    first, second = counts[0, 0], counts[0, 1]
    hot = jnp.where(first > second, 0, 1)
    in_spare = jnp.logical_and(row >= half, row < SUB)
    in_send = row >= 2 * SUB
    expert = jnp.where(in_spare, hot, jnp.where(in_send, 1 - y, y))
    slot = jnp.where(row < half, row, row - half + low)
    slot = jnp.where(row >= SUB, row - SUB - low + half, slot)
    slot = jnp.where(in_send, row - 2 * SUB, slot)
    low_slot = jnp.where(in_send, 0, jnp.where(row < SUB, 0, half))
    high_slot = jnp.where(in_send, low, jnp.where(row < SUB, rows, low))
    valid = jnp.logical_and(slot >= low_slot, slot < high_slot)
    start = jnp.where(expert == 0, 0, first)
    count = jnp.where(expert == 0, first, second)
    take = jnp.logical_and(valid, jnp.logical_and(slot < count, pos == start + slot))
    take = jnp.where(take, 1.0, 0.0).astype(jnp.bfloat16)
    local = lax.broadcasted_iota(jnp.int32, (rows, rows), 0)
    perm = jnp.where(local == route[...], 1.0, 0.0).astype(jnp.bfloat16)
    pick = lax.dot_general(
        take, perm, (((1,), (1,)), ((), ())), preferred_element_type=jnp.float32
    )
    pick_h = pick.astype(jnp.bfloat16)
    pick_g = jnp.where(keep[here] > 0, pick, 0.0).astype(jnp.bfloat16)
    for pick_x, src, x0s, xbs, xys in (
        (pick_g, grad, g0s, gbs, gys),
        (pick_h, hidden, h0s, hbs, hys),
    ):
        cols = xbs.shape[2]
        for part in range(n):
            due.pop(0).wait()
            got = jnp.dot(
                pick_x,
                src[:, part * cols : (part + 1) * cols],
                preferred_element_type=jnp.float32,
            )
            x0s[part, 0, :, 0:cols] = got[:half].astype(jnp.bfloat16)
            x0s[part, 1, :, 0:cols] = got[half:SUB].astype(jnp.bfloat16)
            xbs[part] = got[SUB : 2 * SUB].astype(jnp.bfloat16)
            xys[part] = got[2 * SUB :].astype(jnp.bfloat16)
    mine = jnp.where(hot == y, 1.0, 0.0)
    ones = jnp.ones((half, LANES), jnp.float32)
    for part in range(n):
        g0s[part, 0, :, gcols : gcols + LANES] = ones.astype(jnp.bfloat16)
        g0s[part, 1, :, gcols : gcols + LANES] = (ones * mine).astype(jnp.bfloat16)

    pl.semaphore_wait(barrier, len(peers))

    ends = []

    def send(src, dst, sem, peer, when=None):
        copy = pltpu.make_async_remote_copy(
            src_ref=src,
            dst_ref=dst,
            send_sem=send_sem.at[len(ends)],
            recv_sem=sem,
            device_id=peer,
            device_id_type=MESH,
        )
        ends.append((copy, when))
        if when is None:
            copy.start()
        else:
            pl.when(when)(copy.start)

    def landed(view, sem):
        pltpu.make_async_copy(view, view, sem).wait()

    across = (here, 1 - y)
    beside = (z * n + twin, y)
    upper = (jnp.minimum(z + 1, n - 1) * n + q, y)
    lower = (jnp.maximum(z - 1, 0) * n + q, y)
    hs, gs = (h0, hb), (g0, gb)
    h_own, g_own = (h0s, hbs), (g0s, gbs)
    h_at = lambda b, s, k: h_sem.at[(b * n + s) * n + k]
    g_at = lambda b, s, k: g_sem.at[(b * n + s) * n + k]

    def own_h(b):
        return pltpu.make_async_copy(h_own[b].at[z], hs[b].at[z, q], own_sem.at[2 * b])

    def own_g(b):
        return pltpu.make_async_copy(g_own[b].at[q], gs[b].at[z, q], own_sem.at[2 * b + 1])

    def start_g(b):
        for to in (over, far, twin):
            send(g_own[b].at[to], gs[b].at[z, q], g_at(b, z, q), (z * n + to, y))
        send(g_own[b].at[q], gs[b].at[z, q], g_at(b, z, q), upper, z + 1 < n)
        send(g_own[b].at[q], gs[b].at[z, q], g_at(b, z, q), lower, z >= 1)
        own_g(b).start()

    def start_h(b):
        for d in (1, 3, 2):
            send(h_own[b].at[zs[d]], hs[b].at[z, q], h_at(b, z, q), (zs[d] * n + q, y))
        for to in (over, twin):
            send(h_own[b].at[z], hs[b].at[z, q], h_at(b, z, q), (z * n + to, y))
        own_h(b).start()

    def plane_g(b):
        for k in (twin, over, far):
            view = gs[b].at[z, k]
            landed(view, g_at(b, z, k))
            send(view, view, g_at(b, z, k), upper, z + 1 < n)
            send(view, view, g_at(b, z, k), lower, z >= 1)

    def forward_g(b, d):
        down, up = jnp.maximum(z - d, 0), jnp.minimum(z + d, n - 1)
        for k in (q, twin, over, far):
            under, above = gs[b].at[down, k], gs[b].at[up, k]

            @pl.when(z - d >= 0)
            def _():
                landed(under, g_at(b, down, k))

            if d < n - 1:
                send(under, under, g_at(b, down, k), upper, jnp.logical_and(z + 1 < n, z - d >= 0))

            @pl.when(z + d < n)
            def _():
                landed(above, g_at(b, up, k))

            if d < n - 1:
                send(above, above, g_at(b, up, k), lower, jnp.logical_and(z >= 1, z + d < n))

    def fan_h(b, d):
        view = hs[b].at[zs[d], q]
        landed(view, h_at(b, zs[d], q))
        for to in (over, twin):
            send(view, view, h_at(b, zs[d], q), (z * n + to, y))

    def relay_h(b, d):
        view = hs[b].at[zs[d], over]
        landed(view, h_at(b, zs[d], over))
        send(view, view, h_at(b, zs[d], over), beside)

    def cross_h(d):
        for k in (q, over):
            send(h0.at[zs[d], k, 1], hx.at[zs[d], k], hx_sem.at[zs[d] * n + k], across)

    def cross_g(s):
        send(g0.at[s, :, 1, :, 0:gcols], gx.at[s], gx_sem.at[s], across)

    start_g(0)
    send(gys, gyr, y_sem.at[0], across)
    start_h(0)
    send(hys, hyr, y_sem.at[1], across)
    plane_g(0)
    fan_h(0, 1)
    fan_h(0, 3)
    forward_g(0, 1)
    landed(gyr, y_sem.at[0])
    gbs[...] = gbs[...] + gyr[...]
    start_g(1)
    fan_h(0, 2)
    for d in (0, 1, 3, 2):
        relay_h(0, d)
    forward_g(0, 2)
    landed(hyr, y_sem.at[1])
    hbs[...] = hbs[...] + hyr[...]
    start_h(1)
    own_h(0).wait()
    own_g(0).wait()
    for d in (0, 1, 3, 2):
        cross_h(d)
    cross_g(z)
    plane_g(1)
    forward_g(0, 3)
    for s in zs[1:]:
        cross_g(s)
    for d in (1, 3, 2):
        fan_h(1, d)
    forward_g(1, 1)
    for d in (0, 1, 3, 2):
        relay_h(1, d)
    for c in range(gcols // LANES):
        cut = slice(c * LANES, (c + 1) * LANES)
        g0m[:, :, :, :, cut] = g0[:, :, :, :, cut] * g0[:, :, :, :, gcols : gcols + LANES]
    forward_g(1, 2)
    for s in zs:
        for k in (q, over):
            view = hx.at[s, k]
            landed(view, hx_sem.at[s * n + k])
            send(view, view, hx_sem.at[s * n + k], beside)
    for s in range(n):
        landed(gx.at[s], gx_sem.at[s])
        for c in range(gcols // LANES):
            cut = slice(c * LANES, (c + 1) * LANES)
            gx[s, :, :, cut] = gx[s, :, :, cut] * g0[s, :, 1, :, gcols : gcols + LANES]
    forward_g(1, 3)
    for s in zs:
        for k in (twin, far):
            for b in range(2):
                landed(hs[b].at[s, k], h_at(b, s, k))
            landed(hx.at[s, k], hx_sem.at[s * n + k])
    own_h(1).wait()
    own_g(1).wait()
    for copy, when in ends:
        if when is None:
            copy.wait_send()
        else:
            pl.when(when)(copy.wait_send)


def n_sends(n):
    per_block = 10 + 2 * (n - 1) + 2 * n * (n - 2) + 2 * (n - 1) + n
    return 2 + 2 * per_block + 2 * n + n + 2 * n


def gather_pairs(hidden, out_grad, counts, route_index, keep, capacity):
    replicas = lax.axis_size("dp")
    n = math.isqrt(replicas)
    hcols, gcols = hidden.shape[1] // n, out_grad.shape[1] // n
    half = SUB // 2
    kind = jnp.bfloat16
    vmem = pl.BlockSpec(memory_space=pltpu.VMEM)
    h0, g0, hb, gb, hx, gx = pl.pallas_call(
        functools.partial(spread_kernel, n, hidden.shape[0] - capacity),
        out_shape=[
            jax.ShapeDtypeStruct((n, n, 2, half, hcols), kind),
            jax.ShapeDtypeStruct((n, n, 2, half, gcols), kind),
            jax.ShapeDtypeStruct((n, n, SUB, hcols), kind),
            jax.ShapeDtypeStruct((n, n, SUB, gcols), kind),
            jax.ShapeDtypeStruct((n, n, half, hcols), kind),
            jax.ShapeDtypeStruct((n, n, half, gcols), kind),
        ],
        in_specs=[pl.BlockSpec(memory_space=pltpu.HBM)] * 5,
        out_specs=[vmem] * 6,
        scratch_shapes=[
            pltpu.SMEM(counts.shape, counts.dtype),
            pltpu.SMEM(keep.shape, keep.dtype),
            pltpu.VMEM(route_index.shape, route_index.dtype),
            pltpu.VMEM(hidden.shape, kind),
            pltpu.VMEM(out_grad.shape, kind),
            pltpu.VMEM((n, n, 2, half, gcols + LANES), kind),
            pltpu.VMEM((n, 2, half, hcols), kind),
            pltpu.VMEM((n, 2, half, gcols + LANES), kind),
            pltpu.VMEM((n, SUB, hcols), kind),
            pltpu.VMEM((n, SUB, gcols), kind),
            pltpu.VMEM((n, SUB, hcols), kind),
            pltpu.VMEM((n, SUB, gcols), kind),
            pltpu.VMEM((n, SUB, hcols), kind),
            pltpu.VMEM((n, SUB, gcols), kind),
            pltpu.SemaphoreType.DMA((3 + 2 * n,)),
            pltpu.SemaphoreType.DMA((n_sends(n),)),
            pltpu.SemaphoreType.DMA((2 * n * n,)),
            pltpu.SemaphoreType.DMA((2 * n * n,)),
            pltpu.SemaphoreType.DMA((n * n,)),
            pltpu.SemaphoreType.DMA((n,)),
            pltpu.SemaphoreType.DMA((2,)),
            pltpu.SemaphoreType.DMA((4,)),
        ],
        compiler_params=pltpu.CompilerParams(
            collective_id=0, has_side_effects=True, vmem_limit_bytes=28 << 20
        ),
        name="spread",
    )(*[pltpu.with_memory_space_constraint(x, pltpu.HBM) for x in (counts, keep, route_index, hidden, out_grad)])
    return [
        (h0.reshape(-1, hcols), g0.reshape(-1, gcols)),
        (hb.reshape(-1, hcols), gb.reshape(-1, gcols)),
        (hx.reshape(-1, hcols), gx.reshape(-1, gcols)),
    ]


def tile_kernel(pairs, keep, *refs):
    out, scales = refs[2 * pairs :]
    replicas = keep.shape[0]
    kept = keep[0]
    for i in range(1, replicas):
        kept = kept + keep[i]
    factor = jnp.float32(replicas) / jnp.maximum(
        jnp.full((1, LANES), kept, jnp.int32).astype(jnp.float32), 1.0
    )
    total = None
    for i in range(pairs):
        term = lax.dot_general(
            refs[2 * i][...],
            refs[2 * i + 1][...],
            (((0,), (0,)), ((), ())),
            preferred_element_type=jnp.float32,
        )
        total = term if total is None else total + term
    tops = []
    for b in range(out.shape[1] // LANES):
        block = total[:, b * LANES : (b + 1) * LANES] * factor
        top = jnp.max(jnp.abs(block), axis=1, keepdims=True)
        out[:, b * LANES : (b + 1) * LANES] = block * (1.0 / (top + 1e-6))
        tops.append(top)
    lane = lax.broadcasted_iota(jnp.int32, (out.shape[0], LANES), 1)
    packed = jnp.zeros((out.shape[0], LANES), jnp.float32)
    for b, top in enumerate(tops):
        packed = jnp.where(lane == b, top, packed)
    spun = packed.T
    for b in range(scales.shape[0]):
        scales[b] = spun[b : b + 1]


def tile_grad(pairs, keep):
    rows, cols = pairs[0][0].shape[1], pairs[0][1].shape[1]
    step = min(rows, 512)
    args, specs = [], []
    for h, g in pairs:
        args += [h, g]
        specs.append(pl.BlockSpec((h.shape[0], step), lambda i: (0, i)))
        specs.append(pl.BlockSpec((g.shape[0], cols), lambda i: (0, 0)))
    return pl.pallas_call(
        functools.partial(tile_kernel, len(pairs)),
        grid=(rows // step,),
        out_shape=[
            jax.ShapeDtypeStruct((rows, cols), jnp.float32),
            jax.ShapeDtypeStruct((cols // LANES, 1, rows), jnp.float32),
        ],
        in_specs=[pl.BlockSpec(memory_space=pltpu.SMEM)] + specs,
        out_specs=[
            pl.BlockSpec((step, cols), lambda i: (i, 0)),
            pl.BlockSpec((cols // LANES, 1, step), lambda i: (0, 0, i)),
        ],
        compiler_params=pltpu.CompilerParams(vmem_limit_bytes=32 << 20),
        name="tile_grad",
    )(keep, *args)


def on_device(hidden, out_grad, counts, route_index, keep):
    experts = lax.axis_size("expert")
    tok_rows = hidden.shape[0]
    capacity = max(tok_rows // 4, tok_rows // experts + 4)
    low = tok_rows - capacity
    paired = (
        experts == 2
        and lax.axis_size("dp") == 16
        and low == SUB - 4
        and capacity - low == SUB // 2
    )
    gather = gather_pairs if paired else gather_general
    pairs = gather(hidden, out_grad, counts, route_index, keep, capacity)
    normed, scales = tile_grad(pairs, keep)
    return (normed[None, None], jnp.transpose(scales[None], (0, 2, 3, 1)))


def solution(mesh):
    placed = (
        P(("dp", "expert"), None),
        P(("dp", "expert"), None),
        P(("dp", "expert"), None),
        P(("dp", "expert"), None),
        P(),
    )
    return jax.shard_map(
        on_device,
        mesh=mesh,
        in_specs=placed,
        out_specs=(P("expert", "dp", None, None), P("expert", "dp", None, None)),
        check_vma=False,
    )
```

```python
import functools
import math

import jax
import jax.numpy as jnp
from jax import lax
from jax.experimental import pallas as pl
from jax.experimental.pallas import tpu as pltpu
from jax.sharding import PartitionSpec as P

MESH = pl.DeviceIdType.MESH
LANES = 128
SUB = 16


def swapped(block, axis, bit):
    count = lax.axis_size(axis)
    route = []
    for low in range(count):
        high = low | 1 << bit
        if high != low and high < count:
            route += [(low, high), (high, low)]
    return lax.ppermute(block, axis, route)


def build_slots(rows_dev, counts_dev, perm_dev, capacity):
    ids = jnp.arange(counts_dev.shape[0], dtype=jnp.int32)
    before = ids[None, :] < ids[:, None]
    offsets = jnp.sum(jnp.where(before, counts_dev[None, :], 0), axis=1)
    slots = jnp.arange(capacity, dtype=jnp.int32)
    position = offsets[:, None] + slots[None, :]
    position = jnp.minimum(position, rows_dev.shape[0] - 1)
    live = slots[None, :] < counts_dev[:, None]
    local = perm_dev[position]
    picked = rows_dev[local]
    return jnp.where(live[:, :, None], picked, jnp.zeros_like(picked))


def join_pair(mine, partner, replica, bit):
    lower = replica >> bit & 1 == 0
    first = jnp.concatenate([mine, partner], axis=1)
    second = jnp.concatenate([partner, mine], axis=1)
    return jnp.where(lower, first, second)


def gather_general(hidden, out_grad, counts, route_index, keep, capacity):
    experts = lax.axis_size("expert")
    replicas = lax.axis_size("dp")
    side = math.isqrt(replicas)
    levels = side.bit_length() - 1
    replica = lax.axis_index("dp")
    hidden_units = hidden.shape[1]
    width = out_grad.shape[1]
    grad_rows = jnp.where(keep[replica] > 0, out_grad, jnp.zeros_like(out_grad))
    send_h = build_slots(hidden, counts[0], route_index[0], capacity)
    send_g = build_slots(grad_rows, counts[0], route_index[0], capacity)
    recv_h = lax.all_to_all(send_h, "expert", split_axis=0, concat_axis=0, tiled=True)
    recv_g = lax.all_to_all(send_g, "expert", split_axis=0, concat_axis=0, tiled=True)
    slot_count = experts * capacity
    tile_rows = hidden_units // side
    tile_cols = width // side
    sub_rows = slot_count // side
    piece_h = (
        recv_h.reshape(side, sub_rows, side, tile_rows)
        .transpose(2, 0, 1, 3)
        .reshape(replicas, sub_rows, tile_rows)
    )
    piece_g = (
        recv_g.reshape(side, sub_rows, side, tile_cols)
        .transpose(0, 2, 1, 3)
        .reshape(replicas, sub_rows, tile_cols)
    )
    all_h = lax.all_to_all(piece_h, "dp", split_axis=0, concat_axis=0, tiled=True)
    all_g = lax.all_to_all(piece_g, "dp", split_axis=0, concat_axis=0, tiled=True)
    for bit in range(levels):
        all_h = join_pair(all_h, swapped(all_h, "dp", bit), replica, bit)
    for bit in range(levels, 2 * levels):
        all_g = join_pair(all_g, swapped(all_g, "dp", bit), replica, bit)
    return [(all_h.reshape(-1, tile_rows), all_g.reshape(-1, tile_cols))]


def block_grads(h_ref, g_ref, i, step, factor):
    total = lax.dot_general(
        h_ref[:, pl.ds(pl.multiple_of(i * step, step), step)],
        g_ref[...],
        (((0,), (0,)), ((), ())),
        preferred_element_type=jnp.float32,
    )
    lane = lax.broadcasted_iota(jnp.int32, (step, LANES), 1)
    packed = jnp.zeros((step, LANES), jnp.float32)
    blocks = []
    for b in range(g_ref.shape[1] // LANES):
        block = total[:, b * LANES : (b + 1) * LANES] * factor
        top = jnp.max(jnp.abs(block), axis=1, keepdims=True)
        blocks.append(block * (1.0 / (top + 1e-6)))
        packed = jnp.where(lane == b, top, packed)
    return blocks, packed.T


def spread_kernel(
    n, low, counts_in, keep_in, route_in, hidden_in, grad_in,
    hall, g_left, g_right, done, tops, factor_out,
    counts, keep, route, hidden, grad, h0, g0, hx, gx, h0s, g0s, hbs, gbs, hys, gys, hyr, gyr,
    in_sem, send_sem, h_sem, g_sem, hx_sem, gx_sem, y_sem, own_sem, two_sem, three_sem,
):
    here = lax.axis_index("dp")
    y = lax.axis_index("expert")
    z, q = here // n, here % n
    twin = q + 1 - 2 * (q % 2)
    over = (q + n // 2) % n
    far = (twin + n // 2) % n
    near = jnp.maximum(z - 1, 1 - z)
    last = (n - 1) * (1 - z // 2)
    mid = n * (n - 1) // 2 - z - near - last
    others = (near, mid, last)
    half = SUB // 2
    n_first = n * n * SUB
    n_both = 2 * n_first
    hcols, gcols = hall.shape[1], gx.shape[3]
    side = gcols // 2
    left = z >= 1
    right = z + 1 < n

    moves = []
    for src, dst in ((counts_in, counts), (keep_in, keep), (route_in, route)):
        moves.append(pltpu.make_async_copy(src, dst, in_sem.at[len(moves)]))
    for src, dst in ((grad_in, grad), (hidden_in, hidden)):
        cols = src.shape[1] // n
        for part in range(n):
            cut = (slice(None), pl.ds(part * cols, cols))
            moves.append(pltpu.make_async_copy(src.at[cut], dst.at[cut], in_sem.at[len(moves)]))
    for move in moves:
        move.start()

    across = (here, 1 - y)
    beside = (z * n + twin, y)
    upper = (jnp.minimum(z + 1, n - 1) * n + q, y)
    lower = (jnp.maximum(z - 1, 0) * n + q, y)

    def signal(sem, peer):
        pl.semaphore_signal(sem, inc=1, device_id=peer, device_id_type=MESH)

    barrier = pltpu.get_barrier_semaphore()
    for peer in (across, (z * n + over, y), (z * n + far, y), beside):
        signal(barrier, peer)
    pl.when(right)(lambda: signal(barrier, upper))
    pl.when(left)(lambda: signal(barrier, lower))

    for move in moves[:3]:
        move.wait()
    due = moves[3:]
    rows = hidden.shape[0]
    total = 3 * SUB
    row = lax.broadcasted_iota(jnp.int32, (total, rows), 0)
    pos = lax.broadcasted_iota(jnp.int32, (total, rows), 1)
    first, second = counts[0, 0], counts[0, 1]
    hot = jnp.where(first > second, 0, 1)
    in_spare = jnp.logical_and(row >= half, row < SUB)
    in_send = row >= 2 * SUB
    expert = jnp.where(in_spare, hot, jnp.where(in_send, 1 - y, y))
    slot = jnp.where(row < half, row, row - half + low)
    slot = jnp.where(row >= SUB, row - SUB - low + half, slot)
    slot = jnp.where(in_send, row - 2 * SUB, slot)
    low_slot = jnp.where(in_send, 0, jnp.where(row < SUB, 0, half))
    high_slot = jnp.where(in_send, low, jnp.where(row < SUB, rows, low))
    valid = jnp.logical_and(slot >= low_slot, slot < high_slot)
    start = jnp.where(expert == 0, 0, first)
    count = jnp.where(expert == 0, first, second)
    take = jnp.logical_and(valid, jnp.logical_and(slot < count, pos == start + slot))
    take = jnp.where(take, 1.0, 0.0).astype(jnp.bfloat16)
    local = lax.broadcasted_iota(jnp.int32, (rows, rows), 0)
    perm = jnp.where(local == route[...], 1.0, 0.0).astype(jnp.bfloat16)
    pick = lax.dot_general(
        take, perm, (((1,), (1,)), ((), ())), preferred_element_type=jnp.float32
    )
    pick_h = pick.astype(jnp.bfloat16)
    pick_g = jnp.where(keep[here] > 0, pick, 0.0).astype(jnp.bfloat16)
    for pick_x, src, x0s, xys in ((pick_g, grad, g0s, gys), (pick_h, hidden, h0s, hys)):
        cols = xys.shape[2]
        for part in range(n):
            due.pop(0).wait()
            got = jnp.dot(
                pick_x,
                src[:, part * cols : (part + 1) * cols],
                preferred_element_type=jnp.float32,
            )
            x0s[part, 0, :, 0:cols] = got[:half].astype(jnp.bfloat16)
            x0s[part, 1, :, 0:cols] = got[half:SUB].astype(jnp.bfloat16)
            xys[part] = got[2 * SUB :].astype(jnp.bfloat16)
            rest = got[SUB : 2 * SUB].astype(jnp.bfloat16)
            if x0s is h0s:
                hbs[part] = rest
            else:
                gbs[0, part] = rest[:, :side]
                gbs[1, part] = rest[:, side:]
    mine = jnp.where(hot == y, 1.0, 0.0)
    ones = jnp.ones((half, LANES), jnp.float32)
    for part in range(n):
        g0s[part, 0, :, gcols : gcols + LANES] = ones.astype(jnp.bfloat16)
        g0s[part, 1, :, gcols : gcols + LANES] = (ones * mine).astype(jnp.bfloat16)
    kept = keep[0]
    for i in range(1, n * n):
        kept = kept + keep[i]
    factor = jnp.float32(n * n) / jnp.maximum(
        jnp.full((half, LANES), kept, jnp.int32).astype(jnp.float32), 1.0
    )
    factor_out[...] = factor

    pl.semaphore_wait(barrier, 4 + jnp.minimum(z, 1) + jnp.minimum(n - 1 - z, 1))

    ends = []

    def send(src, dst, sem, peer, when=None):
        copy = pltpu.make_async_remote_copy(
            src_ref=src,
            dst_ref=dst,
            send_sem=send_sem.at[len(ends)],
            recv_sem=sem,
            device_id=peer,
            device_id_type=MESH,
        )
        ends.append((copy, when))
        if when is None:
            copy.start()
        else:
            pl.when(when)(copy.start)

    def landed(view, sem):
        pltpu.make_async_copy(view, view, sem).wait()

    sides = (g_left, g_right)

    def h_view(b, s, k):
        if b == 0:
            return h0.at[s, k]
        return hall.at[pl.ds(pl.multiple_of(n_first + (s * n + k) * SUB, SUB), SUB)]

    def g_view(b, s, k, chunks=1):
        if b == 0:
            return g0.at[s, k]
        at = pl.multiple_of(n_first + (s * n + k) * SUB, SUB)
        return sides[b - 1].at[pl.ds(at, chunks * SUB)]

    h_own = lambda b, k: (h0s, hbs)[b].at[k]
    g_own = lambda b, k: g0s.at[k] if b == 0 else gbs.at[b - 1, k]
    h_at = lambda b, s, k: h_sem.at[(b * n + s) * n + k]
    g_at = lambda b, s, k: g_sem.at[(b * n + s) * n + k]
    chunks = lambda b: [(k, 1) for k in (q, twin, over, far)] if b == 0 else [(q - q % 2, 2), (over - over % 2, 2)]

    def own_h(b):
        return pltpu.make_async_copy(h_own(b, z), h_view(b, z, q), own_sem.at[b])

    def own_g(b):
        return pltpu.make_async_copy(g_own(b, q), g_view(b, z, q), own_sem.at[2 + b])

    def start_g(b):
        for to in (over, far, twin):
            send(g_own(b, to), g_view(b, z, q), g_at(b, z, q), (z * n + to, y))
        own_g(b).start()

    def both_ways(view, sem):
        send(view, view, sem, upper, right)
        send(view, view, sem, lower, left)

    def first_g():
        send(g_own(0, q), g_view(0, z, q), g_at(0, z, q), upper, right)
        send(g_own(0, q), g_view(0, z, q), g_at(0, z, q), lower, left)

    def plane_g(b):
        if b == 0:
            for k in (twin, over, far):
                landed(g_view(b, z, k), g_at(b, z, k))
                both_ways(g_view(b, z, k), g_at(b, z, k))
            return
        own_g(b).wait()
        for pair in ((twin,), (over, far)):
            for k in pair:
                landed(g_view(b, z, k), g_at(b, z, k))
            k = pair[0] - pair[0] % 2
            both_ways(g_view(b, z, k, 2), g_at(b, z, k))

    def start_h(b, d):
        up, down = jnp.minimum(z + d, n - 1), jnp.maximum(z - d, 0)
        send(h_own(b, up), h_view(b, z, q), h_at(b, z, q), (up * n + q, y), z + d < n)
        send(h_own(b, down), h_view(b, z, q), h_at(b, z, q), (down * n + q, y), z - d >= 0)

    def own_fan(b):
        for to in (over, twin):
            send(h_own(b, z), h_view(b, z, q), h_at(b, z, q), (z * n + to, y))
        own_h(b).start()

    def forward_g(b, d):
        down, up = jnp.maximum(z - d, 0), jnp.minimum(z + d, n - 1)
        for k, count in chunks(b):
            for s, peer, when in (
                (down, upper, jnp.logical_and(right, z - d >= 0)),
                (up, lower, jnp.logical_and(left, z + d < n)),
            ):
                view, sem = g_view(b, s, k, count), g_at(b, s, k)
                pl.when(when)(functools.partial(landed, view, sem))
                send(view, view, sem, peer, when)

    def finish_g(b, d):
        down, up = jnp.maximum(z - d, 0), jnp.minimum(z + d, n - 1)
        for k, count in chunks(b):
            for s, when in ((down, z == n - 1), (up, z == 0)):
                pl.when(when)(
                    functools.partial(landed, g_view(b, s, k, count), g_at(b, s, k))
                )

    def fan_h(b, s):
        view, sem = h_view(b, s, q), h_at(b, s, q)
        landed(view, sem)
        for to in (over, twin):
            send(view, view, sem, (z * n + to, y))

    def relay_h(b, s):
        view, sem = h_view(b, s, over), h_at(b, s, over)
        landed(view, sem)
        send(view, view, sem, beside)

    def finish_h(b, s):
        for k in (twin, far):
            landed(h_view(b, s, k), h_at(b, s, k))

    def cross_h(s):
        for k in (q, over):
            send(h0.at[s, k, 1], hx.at[s, k], hx_sem.at[s * n + k], across)

    def cross_g(s):
        send(g0.at[s, :, 1, :, 0:gcols], gx.at[s], gx_sem.at[s], across)

    start_g(0)
    first_g()
    send(gys, gyr, y_sem.at[0], across)
    start_h(0, 1)
    own_fan(0)
    send(hys, hyr, y_sem.at[1], across)
    inner = jnp.logical_and(left, right)

    @pl.when(inner)
    def _():
        signal(two_sem.at[0], upper)
        signal(two_sem.at[1], lower)

    pl.when(z >= 2)(lambda: pl.semaphore_wait(two_sem.at[0], 1))
    pl.when(z + 2 < n)(lambda: pl.semaphore_wait(two_sem.at[1], 1))
    pl.when(jnp.logical_and(z >= 2, right))(lambda: signal(three_sem.at[0], upper))
    pl.when(jnp.logical_and(z + 2 < n, left))(lambda: signal(three_sem.at[1], lower))
    start_h(0, 2)
    plane_g(0)
    pl.when(z >= 3)(lambda: pl.semaphore_wait(three_sem.at[0], 1))
    pl.when(z + 3 < n)(lambda: pl.semaphore_wait(three_sem.at[1], 1))
    start_h(0, 3)
    fan_h(0, near)
    forward_g(0, 1)
    landed(gyr, y_sem.at[0])
    for b in (0, 1):
        gbs[b] = gbs[b] + gyr[:, :, b * side : (b + 1) * side]
        start_g(1 + b)
    fan_h(0, mid)
    fan_h(0, last)
    for s in (z,) + others:
        relay_h(0, s)
    forward_g(0, 2)
    landed(hyr, y_sem.at[1])
    hbs[...] = hbs[...] + hyr[...]
    for d in (1, 2, 3):
        start_h(1, d)
    own_fan(1)
    plane_g(1)
    own_h(0).wait()
    own_g(0).wait()
    for s in (z,) + others:
        cross_h(s)
    cross_g(z)
    for d, s in enumerate(others):
        finish_g(0, d + 1)
        cross_g(s)
    for s in others:
        fan_h(1, s)
    forward_g(1, 1)
    forward_g(1, 2)
    plane_g(2)
    for s in (z,) + others:
        relay_h(1, s)
    for s in (z,) + others:
        finish_h(0, s)
    for s in range(n):
        flat = h0[s].astype(jnp.float32).reshape(n * SUB, hcols)
        hall[s * n * SUB : (s + 1) * n * SUB] = flat.astype(jnp.bfloat16)
        mask = g0[s, :, :, :, gcols : gcols + LANES].astype(jnp.float32)
        for c in range(gcols // LANES):
            at = c * LANES
            part = g0[s, :, :, :, at : at + LANES].astype(jnp.float32) * mask
            part = part.reshape(n * SUB, LANES).astype(jnp.bfloat16)
            to = sides[at // side]
            to[s * n * SUB : (s + 1) * n * SUB, at % side : at % side + LANES] = part
    forward_g(2, 1)
    forward_g(2, 2)
    for s in (z,) + others:
        for k in (q, over):
            view = hx.at[s, k]
            landed(view, hx_sem.at[s * n + k])
            send(view, view, hx_sem.at[s * n + k], beside)
    for s in range(n):
        landed(gx.at[s], gx_sem.at[s])
        mask = g0[s, :, 1, :, gcols : gcols + LANES].astype(jnp.float32)
        at_row = n_both + s * n * half
        for c in range(gcols // LANES):
            at = c * LANES
            part = gx[s, :, :, at : at + LANES].astype(jnp.float32) * mask
            part = part.reshape(n * half, LANES).astype(jnp.bfloat16)
            to = sides[at // side]
            to[at_row : at_row + n * half, at % side : at % side + LANES] = part
    own_h(1).wait()
    for s in (z,) + others:
        finish_h(1, s)
        for k in (twin, far):
            landed(hx.at[s, k], hx_sem.at[s * n + k])
    for s in range(n):
        at_row = n_both + s * n * half
        flat = hx[s].astype(jnp.float32).reshape(n * half, hcols)
        hall[at_row : at_row + n * half] = flat.astype(jnp.bfloat16)
    for d in range(1, n):
        finish_g(1, d)
    step = min(hcols, 512)

    @pl.loop(0, hcols // step)
    def _(i):
        blocks, spun = block_grads(hall, g_left, i, step, factor_out[0:1])
        at = pl.ds(pl.multiple_of(i * step, step), step)
        for b, block in enumerate(blocks):
            done[at, b * LANES : (b + 1) * LANES] = block
            tops[b, :, at] = spun[b : b + 1]

    for d in range(1, n):
        finish_g(2, d)
    for copy, when in ends:
        if when is None:
            copy.wait_send()
        else:
            pl.when(when)(copy.wait_send)


def n_sends(n):
    first = 5 + 2 * (n - 1) + 2 * n * (n - 2)
    h_block = 2 * (n - 1) + 2 + 2 * (n - 1) + n
    g_side = 3 + 4 + 4 * (n - 2)
    return first + 2 * h_block + 2 * g_side + 2 + 2 * n + n + 2 * n


def grad_pairs(hidden, out_grad, counts, route_index, keep, capacity):
    replicas = lax.axis_size("dp")
    n = math.isqrt(replicas)
    hcols, gcols = hidden.shape[1] // n, out_grad.shape[1] // n
    half, side = SUB // 2, gcols // 2
    depth = 2 * n * n * SUB + n * n * half
    kind = jnp.bfloat16
    vmem = pl.BlockSpec(memory_space=pltpu.VMEM)
    made = pl.pallas_call(
        functools.partial(spread_kernel, n, hidden.shape[0] - capacity),
        out_shape=[
            jax.ShapeDtypeStruct((depth, hcols), kind),
            jax.ShapeDtypeStruct((depth, side), kind),
            jax.ShapeDtypeStruct((depth, side), kind),
            jax.ShapeDtypeStruct((hcols, side), jnp.float32),
            jax.ShapeDtypeStruct((side // LANES, 1, hcols), jnp.float32),
            jax.ShapeDtypeStruct((half, LANES), jnp.float32),
        ],
        in_specs=[pl.BlockSpec(memory_space=pltpu.HBM)] * 5,
        out_specs=[vmem] * 6,
        scratch_shapes=[
            pltpu.SMEM(counts.shape, counts.dtype),
            pltpu.SMEM(keep.shape, keep.dtype),
            pltpu.VMEM(route_index.shape, route_index.dtype),
            pltpu.VMEM(hidden.shape, kind),
            pltpu.VMEM(out_grad.shape, kind),
            pltpu.VMEM((n, n, 2, half, hcols), kind),
            pltpu.VMEM((n, n, 2, half, gcols + LANES), kind),
            pltpu.VMEM((n, n, half, hcols), kind),
            pltpu.VMEM((n, n, half, gcols), kind),
            pltpu.VMEM((n, 2, half, hcols), kind),
            pltpu.VMEM((n, 2, half, gcols + LANES), kind),
            pltpu.VMEM((n, SUB, hcols), kind),
            pltpu.VMEM((2, n, SUB, side), kind),
            pltpu.VMEM((n, SUB, hcols), kind),
            pltpu.VMEM((n, SUB, gcols), kind),
            pltpu.VMEM((n, SUB, hcols), kind),
            pltpu.VMEM((n, SUB, gcols), kind),
            pltpu.SemaphoreType.DMA((3 + 2 * n,)),
            pltpu.SemaphoreType.DMA((n_sends(n),)),
            pltpu.SemaphoreType.DMA((2 * n * n,)),
            pltpu.SemaphoreType.DMA((3 * n * n,)),
            pltpu.SemaphoreType.DMA((n * n,)),
            pltpu.SemaphoreType.DMA((n,)),
            pltpu.SemaphoreType.DMA((2,)),
            pltpu.SemaphoreType.DMA((5,)),
            pltpu.SemaphoreType.REGULAR((2,)),
            pltpu.SemaphoreType.REGULAR((2,)),
        ],
        compiler_params=pltpu.CompilerParams(
            collective_id=0, has_side_effects=True, vmem_limit_bytes=36 << 20
        ),
        name="spread",
    )(*[pltpu.with_memory_space_constraint(x, pltpu.HBM) for x in (counts, keep, route_index, hidden, out_grad)])
    hall, _, g_right, done, tops, factor = made
    step = min(hcols, 512)
    return pl.pallas_call(
        functools.partial(last_kernel, step),
        out_shape=[
            jax.ShapeDtypeStruct((hcols, gcols), jnp.float32),
            jax.ShapeDtypeStruct((gcols // LANES, 1, hcols), jnp.float32),
        ],
        in_specs=[vmem] * 5,
        out_specs=[pl.BlockSpec(memory_space=pltpu.HBM), vmem],
        scratch_shapes=[
            pltpu.VMEM((2, step, side), jnp.float32),
            pltpu.SemaphoreType.DMA((2,)),
            pltpu.SemaphoreType.DMA((1,)),
        ],
        compiler_params=pltpu.CompilerParams(vmem_limit_bytes=16 << 20),
        name="last_side",
    )(hall, g_right, done, tops, factor)


def last_kernel(step, hall, g_right, done, tops, factor, out, scales, made, sems, done_sem):
    rows, side = done.shape
    first = pltpu.make_async_copy(done, out.at[:, 0:side], done_sem.at[0])
    first.start()
    scales[0 : tops.shape[0]] = tops[...]

    def leave(i):
        at = pl.ds(pl.multiple_of(i * step, step), step)
        return pltpu.make_async_copy(made.at[i % 2], out.at[at, side : 2 * side], sems.at[i % 2])

    @pl.loop(0, rows // step)
    def _(i):
        @pl.when(i >= 2)
        def _():
            leave(i - 2).wait()

        blocks, spun = block_grads(hall, g_right, i, step, factor[0:1])
        at = pl.ds(pl.multiple_of(i * step, step), step)
        for b, block in enumerate(blocks):
            made[i % 2, :, b * LANES : (b + 1) * LANES] = block
            scales[tops.shape[0] + b, :, at] = spun[b : b + 1]
        leave(i).start()

    for i in range(max(rows // step - 2, 0), rows // step):
        leave(i).wait()
    first.wait()


def tile_kernel(pairs, keep, *refs):
    out, scales = refs[2 * pairs :]
    replicas = keep.shape[0]
    kept = keep[0]
    for i in range(1, replicas):
        kept = kept + keep[i]
    factor = jnp.float32(replicas) / jnp.maximum(
        jnp.full((1, LANES), kept, jnp.int32).astype(jnp.float32), 1.0
    )
    total = None
    for i in range(pairs):
        term = lax.dot_general(
            refs[2 * i][...],
            refs[2 * i + 1][...],
            (((0,), (0,)), ((), ())),
            preferred_element_type=jnp.float32,
        )
        total = term if total is None else total + term
    tops = []
    for b in range(out.shape[1] // LANES):
        block = total[:, b * LANES : (b + 1) * LANES] * factor
        top = jnp.max(jnp.abs(block), axis=1, keepdims=True)
        out[:, b * LANES : (b + 1) * LANES] = block * (1.0 / (top + 1e-6))
        tops.append(top)
    lane = lax.broadcasted_iota(jnp.int32, (out.shape[0], LANES), 1)
    packed = jnp.zeros((out.shape[0], LANES), jnp.float32)
    for b, top in enumerate(tops):
        packed = jnp.where(lane == b, top, packed)
    spun = packed.T
    for b in range(scales.shape[0]):
        scales[b] = spun[b : b + 1]


def tile_grad(pairs, keep):
    rows, cols = pairs[0][0].shape[1], pairs[0][1].shape[1]
    step = min(rows, 512)
    args, specs = [], []
    for h, g in pairs:
        args += [h, g]
        specs.append(pl.BlockSpec((h.shape[0], step), lambda i: (0, i)))
        specs.append(pl.BlockSpec((g.shape[0], cols), lambda i: (0, 0)))
    return pl.pallas_call(
        functools.partial(tile_kernel, len(pairs)),
        grid=(rows // step,),
        out_shape=[
            jax.ShapeDtypeStruct((rows, cols), jnp.float32),
            jax.ShapeDtypeStruct((cols // LANES, 1, rows), jnp.float32),
        ],
        in_specs=[pl.BlockSpec(memory_space=pltpu.SMEM)] + specs,
        out_specs=[
            pl.BlockSpec((step, cols), lambda i: (i, 0)),
            pl.BlockSpec((cols // LANES, 1, step), lambda i: (0, 0, i)),
        ],
        compiler_params=pltpu.CompilerParams(vmem_limit_bytes=32 << 20),
        name="tile_grad",
    )(keep, *args)


def on_device(hidden, out_grad, counts, route_index, keep):
    experts = lax.axis_size("expert")
    tok_rows = hidden.shape[0]
    capacity = max(tok_rows // 4, tok_rows // experts + 4)
    low = tok_rows - capacity
    paired = (
        experts == 2
        and lax.axis_size("dp") == 16
        and low == SUB - 4
        and capacity - low == SUB // 2
    )
    operands = (hidden, out_grad, counts, route_index, keep, capacity)
    if paired:
        normed, scales = grad_pairs(*operands)
    else:
        normed, scales = tile_grad(gather_general(*operands), keep)
    return (normed[None, None], jnp.transpose(scales[None], (0, 2, 3, 1)))


def solution(mesh):
    placed = (
        P(("dp", "expert"), None),
        P(("dp", "expert"), None),
        P(("dp", "expert"), None),
        P(("dp", "expert"), None),
        P(),
    )
    return jax.shard_map(
        on_device,
        mesh=mesh,
        in_specs=placed,
        out_specs=(P("expert", "dp", None, None), P("expert", "dp", None, None)),
        check_vma=False,
    )
```

```python
import functools
import math

import jax
import jax.numpy as jnp
from jax import lax
from jax.experimental import pallas as pl
from jax.experimental.pallas import tpu as pltpu
from jax.sharding import PartitionSpec as P

MESH = pl.DeviceIdType.MESH
LANES = 128
SUB = 16


def swapped(block, axis, bit):
    count = lax.axis_size(axis)
    route = []
    for low in range(count):
        high = low | 1 << bit
        if high != low and high < count:
            route += [(low, high), (high, low)]
    return lax.ppermute(block, axis, route)


def build_slots(rows_dev, counts_dev, perm_dev, capacity):
    ids = jnp.arange(counts_dev.shape[0], dtype=jnp.int32)
    before = ids[None, :] < ids[:, None]
    offsets = jnp.sum(jnp.where(before, counts_dev[None, :], 0), axis=1)
    slots = jnp.arange(capacity, dtype=jnp.int32)
    position = offsets[:, None] + slots[None, :]
    position = jnp.minimum(position, rows_dev.shape[0] - 1)
    live = slots[None, :] < counts_dev[:, None]
    local = perm_dev[position]
    picked = rows_dev[local]
    return jnp.where(live[:, :, None], picked, jnp.zeros_like(picked))


def join_pair(mine, partner, replica, bit):
    lower = replica >> bit & 1 == 0
    first = jnp.concatenate([mine, partner], axis=1)
    second = jnp.concatenate([partner, mine], axis=1)
    return jnp.where(lower, first, second)


def gather_general(hidden, out_grad, counts, route_index, keep, capacity):
    experts = lax.axis_size("expert")
    replicas = lax.axis_size("dp")
    side = math.isqrt(replicas)
    levels = side.bit_length() - 1
    replica = lax.axis_index("dp")
    hidden_units = hidden.shape[1]
    width = out_grad.shape[1]
    grad_rows = jnp.where(keep[replica] > 0, out_grad, jnp.zeros_like(out_grad))
    send_h = build_slots(hidden, counts[0], route_index[0], capacity)
    send_g = build_slots(grad_rows, counts[0], route_index[0], capacity)
    recv_h = lax.all_to_all(send_h, "expert", split_axis=0, concat_axis=0, tiled=True)
    recv_g = lax.all_to_all(send_g, "expert", split_axis=0, concat_axis=0, tiled=True)
    slot_count = experts * capacity
    tile_rows = hidden_units // side
    tile_cols = width // side
    sub_rows = slot_count // side
    piece_h = (
        recv_h.reshape(side, sub_rows, side, tile_rows)
        .transpose(2, 0, 1, 3)
        .reshape(replicas, sub_rows, tile_rows)
    )
    piece_g = (
        recv_g.reshape(side, sub_rows, side, tile_cols)
        .transpose(0, 2, 1, 3)
        .reshape(replicas, sub_rows, tile_cols)
    )
    all_h = lax.all_to_all(piece_h, "dp", split_axis=0, concat_axis=0, tiled=True)
    all_g = lax.all_to_all(piece_g, "dp", split_axis=0, concat_axis=0, tiled=True)
    for bit in range(levels):
        all_h = join_pair(all_h, swapped(all_h, "dp", bit), replica, bit)
    for bit in range(levels, 2 * levels):
        all_g = join_pair(all_g, swapped(all_g, "dp", bit), replica, bit)
    return [(all_h.reshape(-1, tile_rows), all_g.reshape(-1, tile_cols))]


def block_grads(h_ref, g_ref, factor, made, leave):
    step = made.shape[1]
    steps = h_ref.shape[1] // step

    def product(i, slot):
        made[slot] = lax.dot_general(
            h_ref[:, pl.ds(pl.multiple_of(i * step, step), step)],
            g_ref[...],
            (((0,), (0,)), ((), ())),
            preferred_element_type=jnp.float32,
        )

    def normalise(i, slot):
        lane = lax.broadcasted_iota(jnp.int32, (step, LANES), 1)
        packed = jnp.zeros((step, LANES), jnp.float32)
        blocks = []
        for b in range(g_ref.shape[1] // LANES):
            block = made[slot, :, b * LANES : (b + 1) * LANES] * factor
            top = jnp.max(jnp.abs(block), axis=1, keepdims=True)
            blocks.append(block * (1.0 / (top + 1e-6)))
            packed = jnp.where(lane == b, top, packed)
        leave(i, blocks, packed.T)

    product(0, 0)

    @pl.loop(0, steps // 2)
    def _(j):
        product(2 * j + 1, 1)
        normalise(2 * j, 0)
        product(jnp.minimum(2 * j + 2, steps - 1), 0)
        normalise(2 * j + 1, 1)


def spread_kernel(
    n, low, counts_in, keep_in, route_in, hidden_in, grad_in,
    hall, g_left, g_right, done, tops, factor_out,
    counts, keep, route, hidden, grad, h0, g0, hx, gx, h0s, g0s, hbs, gbs, hys, gys, hyr, gyr,
    made, in_sem, send_sem, h_sem, g_sem, hx_sem, gx_sem, y_sem, own_sem, two_sem, three_sem,
):
    here = lax.axis_index("dp")
    y = lax.axis_index("expert")
    z, q = here // n, here % n
    twin = q + 1 - 2 * (q % 2)
    over = (q + n // 2) % n
    far = (twin + n // 2) % n
    mate = z + 1 - 2 * (z % 2)
    jump = (z + 2) % n
    mirror = n - 1 - z
    others = (mate, jump, mirror)
    inner = jnp.logical_and(z >= 1, z + 1 < n)
    half = SUB // 2
    n_first = n * n * SUB
    n_both = 2 * n_first
    hcols, gcols = hall.shape[1], gx.shape[3]
    side = gcols // 2

    moves = []
    for src, dst in ((counts_in, counts), (keep_in, keep), (route_in, route)):
        moves.append(pltpu.make_async_copy(src, dst, in_sem.at[len(moves)]))
    for src, dst in ((grad_in, grad), (hidden_in, hidden)):
        cols = src.shape[1] // n
        for part in range(n):
            cut = (slice(None), pl.ds(part * cols, cols))
            moves.append(pltpu.make_async_copy(src.at[cut], dst.at[cut], in_sem.at[len(moves)]))
    for move in moves:
        move.start()

    across = (here, 1 - y)
    beside = (z * n + twin, y)
    outward = (mate * n + q, y)
    inward = (mirror * n + q, y)

    def signal(sem, peer):
        pl.semaphore_signal(sem, inc=1, device_id=peer, device_id_type=MESH)

    barrier = pltpu.get_barrier_semaphore()
    for peer in (across, (z * n + over, y), (z * n + far, y), beside, outward):
        signal(barrier, peer)
    pl.when(inner)(lambda: signal(barrier, inward))

    for move in moves[:3]:
        move.wait()
    due = moves[3:]
    rows = hidden.shape[0]
    total = 3 * SUB
    row = lax.broadcasted_iota(jnp.int32, (total, rows), 0)
    pos = lax.broadcasted_iota(jnp.int32, (total, rows), 1)
    first, second = counts[0, 0], counts[0, 1]
    hot = jnp.where(first > second, 0, 1)
    in_spare = jnp.logical_and(row >= half, row < SUB)
    in_send = row >= 2 * SUB
    expert = jnp.where(in_spare, hot, jnp.where(in_send, 1 - y, y))
    slot = jnp.where(row < half, row, row - half + low)
    slot = jnp.where(row >= SUB, row - SUB - low + half, slot)
    slot = jnp.where(in_send, row - 2 * SUB, slot)
    low_slot = jnp.where(in_send, 0, jnp.where(row < SUB, 0, half))
    high_slot = jnp.where(in_send, low, jnp.where(row < SUB, rows, low))
    valid = jnp.logical_and(slot >= low_slot, slot < high_slot)
    start = jnp.where(expert == 0, 0, first)
    count = jnp.where(expert == 0, first, second)
    take = jnp.logical_and(valid, jnp.logical_and(slot < count, pos == start + slot))
    take = jnp.where(take, 1.0, 0.0).astype(jnp.bfloat16)
    local = lax.broadcasted_iota(jnp.int32, (rows, rows), 0)
    perm = jnp.where(local == route[...], 1.0, 0.0).astype(jnp.bfloat16)
    pick = lax.dot_general(
        take, perm, (((1,), (1,)), ((), ())), preferred_element_type=jnp.float32
    )
    pick_h = pick.astype(jnp.bfloat16)
    pick_g = jnp.where(keep[here] > 0, pick, 0.0).astype(jnp.bfloat16)

    def pick_rows(pick_x, src, x0s, xys):
        cols = xys.shape[2]
        for part in range(n):
            due.pop(0).wait()
            got = jnp.dot(
                pick_x,
                src[:, part * cols : (part + 1) * cols],
                preferred_element_type=jnp.float32,
            )
            x0s[part, 0, :, 0:cols] = got[:half].astype(jnp.bfloat16)
            x0s[part, 1, :, 0:cols] = got[half:SUB].astype(jnp.bfloat16)
            xys[part] = got[2 * SUB :].astype(jnp.bfloat16)
            rest = got[SUB : 2 * SUB].astype(jnp.bfloat16)
            if x0s is h0s:
                hbs[part] = rest
            else:
                gbs[0, part] = rest[:, :side]
                gbs[1, part] = rest[:, side:]

    mine = jnp.where(hot == y, 1.0, 0.0)
    ones = jnp.ones((half, LANES), jnp.float32)
    for part in range(n):
        g0s[part, 0, :, gcols : gcols + LANES] = ones.astype(jnp.bfloat16)
        g0s[part, 1, :, gcols : gcols + LANES] = (ones * mine).astype(jnp.bfloat16)
    pick_rows(pick_g, grad, g0s, gys)
    enter = 5 + jnp.minimum(z, 1) * jnp.minimum(n - 1 - z, 1)
    pl.semaphore_wait(barrier, enter)

    ends = []

    def send(src, dst, sem, peer, when=None):
        copy = pltpu.make_async_remote_copy(
            src_ref=src,
            dst_ref=dst,
            send_sem=send_sem.at[len(ends)],
            recv_sem=sem,
            device_id=peer,
            device_id_type=MESH,
        )
        ends.append((copy, when))
        if when is None:
            copy.start()
        else:
            pl.when(when)(copy.start)

    def landed(view, sem):
        pltpu.make_async_copy(view, view, sem).wait()

    sides = (g_left, g_right)

    def h_view(b, s, k):
        if b == 0:
            return h0.at[s, k]
        return hall.at[pl.ds(pl.multiple_of(n_first + (s * n + k) * SUB, SUB), SUB)]

    def g_view(b, s, k, chunks=1):
        if b == 0:
            return g0.at[s, k]
        at = pl.multiple_of(n_first + (s * n + k) * SUB, SUB)
        return sides[b - 1].at[pl.ds(at, chunks * SUB)]

    h_own = lambda b, k: (h0s, hbs)[b].at[k]
    g_own = lambda b, k: g0s.at[k] if b == 0 else gbs.at[b - 1, k]
    h_at = lambda b, s, k: h_sem.at[(b * n + s) * n + k]
    g_at = lambda b, s, k: g_sem.at[(b * n + s) * n + k]
    chunks = lambda b: [(k, 1) for k in (q, twin, over, far)] if b == 0 else [(q - q % 2, 2), (over - over % 2, 2)]

    def own_h(b):
        return pltpu.make_async_copy(h_own(b, z), h_view(b, z, q), own_sem.at[b])

    def own_g(b):
        return pltpu.make_async_copy(g_own(b, q), g_view(b, z, q), own_sem.at[2 + b])

    def start_g(b):
        for to in (over, far, twin):
            send(g_own(b, to), g_view(b, z, q), g_at(b, z, q), (z * n + to, y))
        own_g(b).start()

    def both_ways(view, sem):
        send(view, view, sem, outward)
        send(view, view, sem, inward, inner)

    def first_g():
        send(g_own(0, q), g_view(0, z, q), g_at(0, z, q), outward)
        send(g_own(0, q), g_view(0, z, q), g_at(0, z, q), inward, inner)

    def plane_g(b):
        if b == 0:
            for k in (twin, over, far):
                landed(g_view(b, z, k), g_at(b, z, k))
                both_ways(g_view(b, z, k), g_at(b, z, k))
            return
        own_g(b).wait()
        for pair in ((twin,), (over, far)):
            for k in pair:
                landed(g_view(b, z, k), g_at(b, z, k))
            k = pair[0] - pair[0] % 2
            both_ways(g_view(b, z, k, 2), g_at(b, z, k))

    def start_h(b, s):
        send(h_own(b, s), h_view(b, z, q), h_at(b, z, q), (s * n + q, y))

    def own_fan(b):
        for to in (over, twin):
            send(h_own(b, z), h_view(b, z, q), h_at(b, z, q), (z * n + to, y))
        own_h(b).start()

    def forward_g(b, s, peer):
        for k, count in chunks(b):
            view, sem = g_view(b, s, k, count), g_at(b, s, k)
            pl.when(inner)(functools.partial(landed, view, sem))
            send(view, view, sem, peer, inner)

    def forward_near(b):
        forward_g(b, mate, inward)
        forward_g(b, mirror, outward)

    def forward_far(b):
        forward_g(b, jump, outward)

    def finish_g(b, s):
        for k, count in chunks(b):
            pl.when(jnp.logical_not(inner))(
                functools.partial(landed, g_view(b, s, k, count), g_at(b, s, k))
            )

    def fan_h(b, s):
        view, sem = h_view(b, s, q), h_at(b, s, q)
        landed(view, sem)
        for to in (over, twin):
            send(view, view, sem, (z * n + to, y))

    def relay_h(b, s):
        view, sem = h_view(b, s, over), h_at(b, s, over)
        landed(view, sem)
        send(view, view, sem, beside)

    def finish_h(b, s):
        for k in (twin, far):
            landed(h_view(b, s, k), h_at(b, s, k))

    def cross_h(s):
        for k in (q, over):
            send(h0.at[s, k, 1], hx.at[s, k], hx_sem.at[s * n + k], across)

    def cross_g(s):
        send(g0.at[s, :, 1, :, 0:gcols], gx.at[s], gx_sem.at[s], across)

    start_g(0)
    first_g()
    send(gys, gyr, y_sem.at[0], across)

    @pl.when(inner)
    def _():
        signal(two_sem, outward)
        signal(two_sem, inward)

    pick_rows(pick_h, hidden, h0s, hys)
    start_h(0, mate)
    send(h_own(0, mirror), h_view(0, z, q), h_at(0, z, q), inward, inner)
    own_fan(0)
    send(hys, hyr, y_sem.at[1], across)
    plane_g(0)
    pl.semaphore_wait(two_sem, 1)
    pl.when(inner)(lambda: signal(three_sem, outward))
    start_h(0, jump)
    fan_h(0, mate)
    pl.when(jnp.logical_not(inner))(lambda: pl.semaphore_wait(three_sem, 1))
    send(h_own(0, mirror), h_view(0, z, q), h_at(0, z, q), inward, jnp.logical_not(inner))
    forward_near(0)
    landed(gyr, y_sem.at[0])
    for b in (0, 1):
        gbs[b] = gbs[b] + gyr[:, :, b * side : (b + 1) * side]
        start_g(1 + b)
    fan_h(0, jump)
    fan_h(0, mirror)
    for s in (z,) + others:
        relay_h(0, s)
    landed(hyr, y_sem.at[1])
    hbs[...] = hbs[...] + hyr[...]
    for s in others:
        start_h(1, s)
    own_fan(1)
    forward_far(0)
    plane_g(1)
    own_h(0).wait()
    own_g(0).wait()
    for s in (z,) + others:
        cross_h(s)
    cross_g(z)
    for s in others:
        finish_g(0, s)
        cross_g(s)
    fan_h(1, mate)
    forward_near(1)
    plane_g(2)
    fan_h(1, jump)
    fan_h(1, mirror)
    forward_far(1)
    forward_near(2)
    for s in (z,) + others:
        relay_h(1, s)
    forward_far(2)
    kept = keep[0]
    for i in range(1, n * n):
        kept = kept + keep[i]
    factor_out[...] = jnp.float32(n * n) / jnp.maximum(
        jnp.full((half, LANES), kept, jnp.int32).astype(jnp.float32), 1.0
    )
    for s in (z,) + others:
        finish_h(0, s)
    for s in range(n):
        flat = h0[s].astype(jnp.float32).reshape(n * SUB, hcols)
        hall[s * n * SUB : (s + 1) * n * SUB] = flat.astype(jnp.bfloat16)
        mask = g0[s, :, :, :, gcols : gcols + LANES].astype(jnp.float32)
        for c in range(gcols // LANES):
            at = c * LANES
            part = g0[s, :, :, :, at : at + LANES].astype(jnp.float32) * mask
            part = part.reshape(n * SUB, LANES).astype(jnp.bfloat16)
            to = sides[at // side]
            to[s * n * SUB : (s + 1) * n * SUB, at % side : at % side + LANES] = part
    for s in (z,) + others:
        for k in (q, over):
            view = hx.at[s, k]
            landed(view, hx_sem.at[s * n + k])
            send(view, view, hx_sem.at[s * n + k], beside)
    for s in range(n):
        landed(gx.at[s], gx_sem.at[s])
        mask = g0[s, :, 1, :, gcols : gcols + LANES].astype(jnp.float32)
        at_row = n_both + s * n * half
        for c in range(gcols // LANES):
            at = c * LANES
            part = gx[s, :, :, at : at + LANES].astype(jnp.float32) * mask
            part = part.reshape(n * half, LANES).astype(jnp.bfloat16)
            to = sides[at // side]
            to[at_row : at_row + n * half, at % side : at % side + LANES] = part
    own_h(1).wait()
    for s in (z,) + others:
        finish_h(1, s)
        for k in (twin, far):
            landed(hx.at[s, k], hx_sem.at[s * n + k])
    for s in range(n):
        at_row = n_both + s * n * half
        flat = hx[s].astype(jnp.float32).reshape(n * half, hcols)
        hall[at_row : at_row + n * half] = flat.astype(jnp.bfloat16)
    for s in others:
        finish_g(1, s)
    step = made.shape[1]

    def leave(i, blocks, spun):
        at = pl.ds(pl.multiple_of(i * step, step), step)
        for b, block in enumerate(blocks):
            done[at, b * LANES : (b + 1) * LANES] = block
            tops[b, :, at] = spun[b : b + 1]

    block_grads(hall, g_left, factor_out[0:1], made, leave)
    for s in others:
        finish_g(2, s)
    for copy, when in ends:
        if when is None:
            copy.wait_send()
        else:
            pl.when(when)(copy.wait_send)


def n_sends(n):
    first = 5 + 2 * (n - 1) + n * (n - 1)
    h_block = (n - 1) + 2 + 2 * (n - 1) + n
    g_side = 3 + 4 + 2 * (n - 1)
    return first + 2 * h_block + 1 + 2 * g_side + 2 + 2 * n + n + 2 * n


def grad_pairs(hidden, out_grad, counts, route_index, keep, capacity):
    replicas = lax.axis_size("dp")
    n = math.isqrt(replicas)
    hcols, gcols = hidden.shape[1] // n, out_grad.shape[1] // n
    half, side = SUB // 2, gcols // 2
    depth = 2 * n * n * SUB + n * n * half
    step = min(hcols, 512)
    kind = jnp.bfloat16
    vmem = pl.BlockSpec(memory_space=pltpu.VMEM)
    made = pl.pallas_call(
        functools.partial(spread_kernel, n, hidden.shape[0] - capacity),
        out_shape=[
            jax.ShapeDtypeStruct((depth, hcols), kind),
            jax.ShapeDtypeStruct((depth, side), kind),
            jax.ShapeDtypeStruct((depth, side), kind),
            jax.ShapeDtypeStruct((hcols, side), jnp.float32),
            jax.ShapeDtypeStruct((side // LANES, 1, hcols), jnp.float32),
            jax.ShapeDtypeStruct((half, LANES), jnp.float32),
        ],
        in_specs=[pl.BlockSpec(memory_space=pltpu.HBM)] * 5,
        out_specs=[vmem] * 6,
        scratch_shapes=[
            pltpu.SMEM(counts.shape, counts.dtype),
            pltpu.SMEM(keep.shape, keep.dtype),
            pltpu.VMEM(route_index.shape, route_index.dtype),
            pltpu.VMEM(hidden.shape, kind),
            pltpu.VMEM(out_grad.shape, kind),
            pltpu.VMEM((n, n, 2, half, hcols), kind),
            pltpu.VMEM((n, n, 2, half, gcols + LANES), kind),
            pltpu.VMEM((n, n, half, hcols), kind),
            pltpu.VMEM((n, n, half, gcols), kind),
            pltpu.VMEM((n, 2, half, hcols), kind),
            pltpu.VMEM((n, 2, half, gcols + LANES), kind),
            pltpu.VMEM((n, SUB, hcols), kind),
            pltpu.VMEM((2, n, SUB, side), kind),
            pltpu.VMEM((n, SUB, hcols), kind),
            pltpu.VMEM((n, SUB, gcols), kind),
            pltpu.VMEM((n, SUB, hcols), kind),
            pltpu.VMEM((n, SUB, gcols), kind),
            pltpu.VMEM((2, step, side), jnp.float32),
            pltpu.SemaphoreType.DMA((3 + 2 * n,)),
            pltpu.SemaphoreType.DMA((n_sends(n),)),
            pltpu.SemaphoreType.DMA((2 * n * n,)),
            pltpu.SemaphoreType.DMA((3 * n * n,)),
            pltpu.SemaphoreType.DMA((n * n,)),
            pltpu.SemaphoreType.DMA((n,)),
            pltpu.SemaphoreType.DMA((2,)),
            pltpu.SemaphoreType.DMA((5,)),
            pltpu.SemaphoreType.REGULAR,
            pltpu.SemaphoreType.REGULAR,
        ],
        compiler_params=pltpu.CompilerParams(
            collective_id=0, has_side_effects=True, vmem_limit_bytes=36 << 20
        ),
        name="spread",
    )(*[pltpu.with_memory_space_constraint(x, pltpu.HBM) for x in (counts, keep, route_index, hidden, out_grad)])
    hall, _, g_right, done, tops, factor = made
    return pl.pallas_call(
        functools.partial(last_kernel, step),
        out_shape=[
            jax.ShapeDtypeStruct((hcols, gcols), jnp.float32),
            jax.ShapeDtypeStruct((gcols // LANES, 1, hcols), jnp.float32),
        ],
        in_specs=[vmem] * 5,
        out_specs=[pl.BlockSpec(memory_space=pltpu.HBM), vmem],
        scratch_shapes=[
            pltpu.VMEM((2, step, side), jnp.float32),
            pltpu.VMEM((hcols, side), jnp.float32),
            pltpu.SemaphoreType.DMA((hcols // step,)),
            pltpu.SemaphoreType.DMA((1,)),
        ],
        compiler_params=pltpu.CompilerParams(vmem_limit_bytes=20 << 20),
        name="last_side",
    )(hall, g_right, done, tops, factor)


def last_kernel(step, hall, g_right, done, tops, factor, out, scales, made, left, sems, done_sem):
    rows, side = done.shape
    first = pltpu.make_async_copy(done, out.at[:, 0:side], done_sem.at[0])
    first.start()
    scales[0 : tops.shape[0]] = tops[...]

    def away(i):
        at = pl.ds(pl.multiple_of(i * step, step), step)
        return pltpu.make_async_copy(left.at[at], out.at[at, side : 2 * side], sems.at[i])

    def leave(i, blocks, spun):
        at = pl.ds(pl.multiple_of(i * step, step), step)
        for b, block in enumerate(blocks):
            left[at, b * LANES : (b + 1) * LANES] = block
            scales[tops.shape[0] + b, :, at] = spun[b : b + 1]
        away(i).start()

    block_grads(hall, g_right, factor[0:1], made, leave)
    for i in range(rows // step):
        away(i).wait()
    first.wait()


def tile_kernel(pairs, keep, *refs):
    out, scales = refs[2 * pairs :]
    replicas = keep.shape[0]
    kept = keep[0]
    for i in range(1, replicas):
        kept = kept + keep[i]
    factor = jnp.float32(replicas) / jnp.maximum(
        jnp.full((1, LANES), kept, jnp.int32).astype(jnp.float32), 1.0
    )
    total = None
    for i in range(pairs):
        term = lax.dot_general(
            refs[2 * i][...],
            refs[2 * i + 1][...],
            (((0,), (0,)), ((), ())),
            preferred_element_type=jnp.float32,
        )
        total = term if total is None else total + term
    tops = []
    for b in range(out.shape[1] // LANES):
        block = total[:, b * LANES : (b + 1) * LANES] * factor
        top = jnp.max(jnp.abs(block), axis=1, keepdims=True)
        out[:, b * LANES : (b + 1) * LANES] = block * (1.0 / (top + 1e-6))
        tops.append(top)
    lane = lax.broadcasted_iota(jnp.int32, (out.shape[0], LANES), 1)
    packed = jnp.zeros((out.shape[0], LANES), jnp.float32)
    for b, top in enumerate(tops):
        packed = jnp.where(lane == b, top, packed)
    spun = packed.T
    for b in range(scales.shape[0]):
        scales[b] = spun[b : b + 1]


def tile_grad(pairs, keep):
    rows, cols = pairs[0][0].shape[1], pairs[0][1].shape[1]
    step = min(rows, 512)
    args, specs = [], []
    for h, g in pairs:
        args += [h, g]
        specs.append(pl.BlockSpec((h.shape[0], step), lambda i: (0, i)))
        specs.append(pl.BlockSpec((g.shape[0], cols), lambda i: (0, 0)))
    return pl.pallas_call(
        functools.partial(tile_kernel, len(pairs)),
        grid=(rows // step,),
        out_shape=[
            jax.ShapeDtypeStruct((rows, cols), jnp.float32),
            jax.ShapeDtypeStruct((cols // LANES, 1, rows), jnp.float32),
        ],
        in_specs=[pl.BlockSpec(memory_space=pltpu.SMEM)] + specs,
        out_specs=[
            pl.BlockSpec((step, cols), lambda i: (i, 0)),
            pl.BlockSpec((cols // LANES, 1, step), lambda i: (0, 0, i)),
        ],
        compiler_params=pltpu.CompilerParams(vmem_limit_bytes=32 << 20),
        name="tile_grad",
    )(keep, *args)


def on_device(hidden, out_grad, counts, route_index, keep):
    experts = lax.axis_size("expert")
    tok_rows = hidden.shape[0]
    capacity = max(tok_rows // 4, tok_rows // experts + 4)
    low = tok_rows - capacity
    paired = (
        experts == 2
        and lax.axis_size("dp") == 16
        and low == SUB - 4
        and capacity - low == SUB // 2
    )
    operands = (hidden, out_grad, counts, route_index, keep, capacity)
    if paired:
        normed, scales = grad_pairs(*operands)
    else:
        normed, scales = tile_grad(gather_general(*operands), keep)
    return (normed[None, None], jnp.transpose(scales[None], (0, 2, 3, 1)))


def solution(mesh):
    placed = (
        P(("dp", "expert"), None),
        P(("dp", "expert"), None),
        P(("dp", "expert"), None),
        P(("dp", "expert"), None),
        P(),
    )
    return jax.shard_map(
        on_device,
        mesh=mesh,
        in_specs=placed,
        out_specs=(P("expert", "dp", None, None), P("expert", "dp", None, None)),
        check_vma=False,
    )
```

```python
import functools
import math

import jax
import jax.numpy as jnp
from jax import lax
from jax.experimental import pallas as pl
from jax.experimental.pallas import tpu as pltpu
from jax.sharding import PartitionSpec as P

MESH = pl.DeviceIdType.MESH
LANES = 128
SUB = 16


def swapped(block, axis, bit):
    count = lax.axis_size(axis)
    route = []
    for low in range(count):
        high = low | 1 << bit
        if high != low and high < count:
            route += [(low, high), (high, low)]
    return lax.ppermute(block, axis, route)


def build_slots(rows_dev, counts_dev, perm_dev, capacity):
    ids = jnp.arange(counts_dev.shape[0], dtype=jnp.int32)
    before = ids[None, :] < ids[:, None]
    offsets = jnp.sum(jnp.where(before, counts_dev[None, :], 0), axis=1)
    slots = jnp.arange(capacity, dtype=jnp.int32)
    position = offsets[:, None] + slots[None, :]
    position = jnp.minimum(position, rows_dev.shape[0] - 1)
    live = slots[None, :] < counts_dev[:, None]
    local = perm_dev[position]
    picked = rows_dev[local]
    return jnp.where(live[:, :, None], picked, jnp.zeros_like(picked))


def join_pair(mine, partner, replica, bit):
    lower = replica >> bit & 1 == 0
    first = jnp.concatenate([mine, partner], axis=1)
    second = jnp.concatenate([partner, mine], axis=1)
    return jnp.where(lower, first, second)


def gather_general(hidden, out_grad, counts, route_index, keep, capacity):
    experts = lax.axis_size("expert")
    replicas = lax.axis_size("dp")
    side = math.isqrt(replicas)
    levels = side.bit_length() - 1
    replica = lax.axis_index("dp")
    hidden_units = hidden.shape[1]
    width = out_grad.shape[1]
    grad_rows = jnp.where(keep[replica] > 0, out_grad, jnp.zeros_like(out_grad))
    send_h = build_slots(hidden, counts[0], route_index[0], capacity)
    send_g = build_slots(grad_rows, counts[0], route_index[0], capacity)
    recv_h = lax.all_to_all(send_h, "expert", split_axis=0, concat_axis=0, tiled=True)
    recv_g = lax.all_to_all(send_g, "expert", split_axis=0, concat_axis=0, tiled=True)
    slot_count = experts * capacity
    tile_rows = hidden_units // side
    tile_cols = width // side
    sub_rows = slot_count // side
    piece_h = (
        recv_h.reshape(side, sub_rows, side, tile_rows)
        .transpose(2, 0, 1, 3)
        .reshape(replicas, sub_rows, tile_rows)
    )
    piece_g = (
        recv_g.reshape(side, sub_rows, side, tile_cols)
        .transpose(0, 2, 1, 3)
        .reshape(replicas, sub_rows, tile_cols)
    )
    all_h = lax.all_to_all(piece_h, "dp", split_axis=0, concat_axis=0, tiled=True)
    all_g = lax.all_to_all(piece_g, "dp", split_axis=0, concat_axis=0, tiled=True)
    for bit in range(levels):
        all_h = join_pair(all_h, swapped(all_h, "dp", bit), replica, bit)
    for bit in range(levels, 2 * levels):
        all_g = join_pair(all_g, swapped(all_g, "dp", bit), replica, bit)
    return [(all_h.reshape(-1, tile_rows), all_g.reshape(-1, tile_cols))]


def block_grads(h_ref, g_ref, factor, made, leave):
    step = made.shape[1]
    steps = h_ref.shape[1] // step

    def product(i, slot):
        made[slot] = lax.dot_general(
            h_ref[:, pl.ds(pl.multiple_of(i * step, step), step)],
            g_ref[...],
            (((0,), (0,)), ((), ())),
            preferred_element_type=jnp.float32,
        )

    def normalise(i, slot):
        lane = lax.broadcasted_iota(jnp.int32, (step, LANES), 1)
        packed = jnp.zeros((step, LANES), jnp.float32)
        blocks = []
        for b in range(g_ref.shape[1] // LANES):
            block = made[slot, :, b * LANES : (b + 1) * LANES] * factor
            top = jnp.max(jnp.abs(block), axis=1, keepdims=True)
            blocks.append(block * (1.0 / (top + 1e-6)))
            packed = jnp.where(lane == b, top, packed)
        leave(i, blocks, packed.T)

    product(0, 0)

    @pl.loop(0, steps // 2)
    def _(j):
        product(2 * j + 1, 1)
        normalise(2 * j, 0)
        product(jnp.minimum(2 * j + 2, steps - 1), 0)
        normalise(2 * j + 1, 1)


def spread_kernel(
    n, low, counts_in, keep_in, route_in, hidden_in, grad_in,
    hall, g_left, g_right, done, tops, factor_out,
    counts, keep, route, hidden, grad, h0, g0, hx, gx, h0s, g0s, hbs, gbs, hys, gys, hyr, gyr,
    made, in_sem, send_sem, h_sem, g_sem, hx_sem, gx_sem, y_sem, fin_sem, own_sem, two_sem, three_sem,
):
    here = lax.axis_index("dp")
    y = lax.axis_index("expert")
    z, q = here // n, here % n
    twin = q + 1 - 2 * (q % 2)
    over = (q + n // 2) % n
    far = (twin + n // 2) % n
    mate = z + 1 - 2 * (z % 2)
    jump = (z + 2) % n
    mirror = n - 1 - z
    others = (mate, jump, mirror)
    inner = jnp.logical_and(z >= 1, z + 1 < n)
    half = SUB // 2
    n_first = n * n * SUB
    n_both = 2 * n_first
    hcols, gcols = hall.shape[1], gx.shape[3]
    side = gcols // 2

    across = (here, 1 - y)
    beside = (z * n + twin, y)
    outward = (mate * n + q, y)
    inward = (mirror * n + q, y)

    def signal(sem, peer):
        pl.semaphore_signal(sem, inc=1, device_id=peer, device_id_type=MESH)

    barrier = pltpu.get_barrier_semaphore()
    for peer in (across, (z * n + over, y), (z * n + far, y), beside, outward):
        signal(barrier, peer)
    pl.when(inner)(lambda: signal(barrier, inward))

    moves = []
    for src, dst in ((counts_in, counts), (keep_in, keep), (route_in, route)):
        moves.append(pltpu.make_async_copy(src, dst, in_sem.at[len(moves)]))
    for src, dst in ((grad_in, grad), (hidden_in, hidden)):
        cols = src.shape[1] // n
        for part in range(n):
            cut = (slice(None), pl.ds(part * cols, cols))
            moves.append(pltpu.make_async_copy(src.at[cut], dst.at[cut], in_sem.at[len(moves)]))
    for move in moves:
        move.start()

    for move in moves[:3]:
        move.wait()
    due = moves[3:]
    rows = hidden.shape[0]
    total = 3 * SUB
    row = lax.broadcasted_iota(jnp.int32, (total, rows), 0)
    pos = lax.broadcasted_iota(jnp.int32, (total, rows), 1)
    first, second = counts[0, 0], counts[0, 1]
    hot = jnp.where(first > second, 0, 1)
    in_spare = jnp.logical_and(row >= half, row < SUB)
    in_send = row >= 2 * SUB
    expert = jnp.where(in_spare, hot, jnp.where(in_send, 1 - y, y))
    slot = jnp.where(row < half, row, row - half + low)
    slot = jnp.where(row >= SUB, row - SUB - low + half, slot)
    slot = jnp.where(in_send, row - 2 * SUB, slot)
    low_slot = jnp.where(in_send, 0, jnp.where(row < SUB, 0, half))
    high_slot = jnp.where(in_send, low, jnp.where(row < SUB, rows, low))
    valid = jnp.logical_and(slot >= low_slot, slot < high_slot)
    start = jnp.where(expert == 0, 0, first)
    count = jnp.where(expert == 0, first, second)
    take = jnp.logical_and(valid, jnp.logical_and(slot < count, pos == start + slot))
    take = jnp.where(take, 1.0, 0.0).astype(jnp.bfloat16)
    local = lax.broadcasted_iota(jnp.int32, (rows, rows), 0)
    perm = jnp.where(local == route[...], 1.0, 0.0).astype(jnp.bfloat16)
    pick = lax.dot_general(
        take, perm, (((1,), (1,)), ((), ())), preferred_element_type=jnp.float32
    )
    pick_h = pick.astype(jnp.bfloat16)
    pick_g = jnp.where(keep[here] > 0, pick, 0.0).astype(jnp.bfloat16)

    def pick_rows(pick_x, src, x0s, xys):
        cols = xys.shape[2]
        for part in range(n):
            due.pop(0).wait()
            got = jnp.dot(
                pick_x,
                src[:, part * cols : (part + 1) * cols],
                preferred_element_type=jnp.float32,
            )
            x0s[part, 0, :, 0:cols] = got[:half].astype(jnp.bfloat16)
            x0s[part, 1, :, 0:cols] = got[half:SUB].astype(jnp.bfloat16)
            xys[part] = got[2 * SUB :].astype(jnp.bfloat16)
            rest = got[SUB : 2 * SUB].astype(jnp.bfloat16)
            if x0s is h0s:
                hbs[part] = rest
            else:
                gbs[0, part] = rest[:, :side]
                gbs[1, part] = rest[:, side:]

    mine = jnp.ones((half, LANES), jnp.float32) * jnp.where(hot == y, 1.0, 0.0)
    for part in range(n):
        h0s[part, 0, :, hcols : hcols + LANES] = jnp.ones((half, LANES), jnp.bfloat16)
        h0s[part, 1, :, hcols : hcols + LANES] = mine.astype(jnp.bfloat16)
    pick_rows(pick_g, grad, g0s, gys)
    enter = 5 + jnp.minimum(z, 1) * jnp.minimum(n - 1 - z, 1)
    pl.semaphore_wait(barrier, enter)

    sent = [0] * 5

    def send(src, dst, sem, peer, when=None, group=0, again=False):
        if not again:
            sent[group] += math.prod(src.shape)
        copy = pltpu.make_async_remote_copy(
            src_ref=src,
            dst_ref=dst,
            send_sem=send_sem.at[group],
            recv_sem=sem,
            device_id=peer,
            device_id_type=MESH,
        )
        if when is None:
            copy.start()
        else:
            pl.when(when)(copy.start)

    def landed(view, sem):
        pltpu.make_async_copy(view, view, sem).wait()

    sides = (g_left, g_right)

    def h_view(b, s, k):
        if b == 0:
            return h0.at[s, k]
        return hall.at[pl.ds(pl.multiple_of(n_first + (s * n + k) * SUB, SUB), SUB)]

    def g_view(b, s, k, chunks=1):
        if b == 0:
            return g0.at[s, k]
        at = pl.multiple_of(n_first + (s * n + k) * SUB, SUB)
        return sides[b - 1].at[pl.ds(at, chunks * SUB)]

    h_own = lambda b, k: (h0s, hbs)[b].at[k]
    g_own = lambda b, k: g0s.at[k] if b == 0 else gbs.at[b - 1, k]
    h_at = lambda b, s: h_sem.at[2 * n * b + s]
    h_over = lambda b, s: h_sem.at[2 * n * b + n + s]
    g_at = lambda b, s, k: g_sem.at[(b * n + s) * n + k]
    chunks = lambda b: [(k, 1) for k in (q, twin, over, far)] if b == 0 else [(q - q % 2, 2), (over - over % 2, 2)]

    def own_h(b):
        return pltpu.make_async_copy(h_own(b, z), h_view(b, z, q), own_sem.at[b])

    def own_g(b):
        return pltpu.make_async_copy(g_own(b, q), g_view(b, z, q), own_sem.at[2 + b])

    def start_g(b):
        for to in (over, far, twin):
            send(g_own(b, to), g_view(b, z, q), g_at(b, z, q), (z * n + to, y))
        own_g(b).start()

    def both_ways(view, sem):
        send(view, view, sem, outward)
        send(view, view, sem, inward, inner, 1)

    def first_g():
        send(g_own(0, q), g_view(0, z, q), g_at(0, z, q), outward)
        send(g_own(0, q), g_view(0, z, q), g_at(0, z, q), inward, inner, 1)

    def plane_g(b):
        if b == 0:
            for k in (twin, over, far):
                landed(g_view(b, z, k), g_at(b, z, k))
                both_ways(g_view(b, z, k), g_at(b, z, k))
            return
        own_g(b).wait()
        for pair in ((twin,), (over, far)):
            for k in pair:
                landed(g_view(b, z, k), g_at(b, z, k))
            k = pair[0] - pair[0] % 2
            both_ways(g_view(b, z, k, 2), g_at(b, z, k))

    def start_h(b, s, when=None, again=False):
        to = (s * n + q, y)
        send(h_own(b, s), h_view(b, z, q), h_at(b, z), to, when, 0 if b else 2, again)

    def own_fan(b):
        group = 0 if b else 3
        send(h_own(b, z), h_view(b, z, q), h_over(b, z), (z * n + over, y), None, group)
        send(h_own(b, z), h_view(b, z, q), fin_sem.at[b], beside, None, group)
        own_h(b).start()

    def forward_g(b, s, peer):
        for k, count in chunks(b):
            view, sem = g_view(b, s, k, count), g_at(b, s, k)
            pl.when(inner)(functools.partial(landed, view, sem))
            send(view, view, sem, peer, inner, 1)

    def forward_near(b):
        forward_g(b, mate, inward)
        forward_g(b, mirror, outward)

    def forward_far(b):
        forward_g(b, jump, outward)

    def finish_g(b, s):
        for k, count in chunks(b):
            pl.when(jnp.logical_not(inner))(
                functools.partial(landed, g_view(b, s, k, count), g_at(b, s, k))
            )

    def fan_h(b, s):
        view, group = h_view(b, s, q), 0 if b else 3
        landed(view, h_at(b, s))
        send(view, view, h_over(b, s), (z * n + over, y), None, group)
        send(view, view, fin_sem.at[b], beside, None, group)

    def relay_h(b, s):
        view = h_view(b, s, over)
        landed(view, h_over(b, s))
        send(view, view, fin_sem.at[b], beside, None, 0 if b else 4)

    def cross_h(s):
        for j, k in enumerate((q, over)):
            send(h0.at[s, k, 1, :, 0:hcols], hx.at[s, k], hx_sem.at[j * n + s], across)

    def cross_g(s):
        send(g0.at[s, :, 1, :, 0:gcols], gx.at[s], gx_sem.at[s], across)

    start_g(0)
    first_g()
    send(gys, gyr, y_sem.at[0], across)

    @pl.when(inner)
    def _():
        signal(two_sem, outward)
        signal(two_sem, inward)

    pick_rows(pick_h, hidden, h0s, hys)
    start_h(0, mate)
    start_h(0, mirror, inner)
    own_fan(0)
    send(hys, hyr, y_sem.at[1], across)
    plane_g(0)
    pl.semaphore_wait(two_sem, 1)
    pl.when(inner)(lambda: signal(three_sem, outward))
    start_h(0, jump)
    fan_h(0, mate)
    pl.when(jnp.logical_not(inner))(lambda: pl.semaphore_wait(three_sem, 1))
    start_h(0, mirror, jnp.logical_not(inner), True)
    forward_near(0)
    landed(gyr, y_sem.at[0])
    for b in (0, 1):
        gbs[b] = gbs[b] + gyr[:, :, b * side : (b + 1) * side]
        start_g(1 + b)
    fan_h(0, jump)
    fan_h(0, mirror)
    for s in (z,) + others:
        relay_h(0, s)
    landed(hyr, y_sem.at[1])
    hbs[...] = hbs[...] + hyr[...]
    for s in others:
        start_h(1, s)
    own_fan(1)
    own_h(0).wait()
    own_g(0).wait()
    cross_h(z)
    cross_g(z)
    finish_g(0, mate)
    cross_h(mate)
    cross_g(mate)
    forward_far(0)
    plane_g(1)
    for s in (jump, mirror):
        cross_h(s)
        finish_g(0, s)
        cross_g(s)
    fan_h(1, mate)
    forward_near(1)
    plane_g(2)
    fan_h(1, jump)
    fan_h(1, mirror)
    forward_far(1)
    kept = keep[0]
    for i in range(1, n * n):
        kept = kept + keep[i]
    factor_out[...] = jnp.float32(n * n) / jnp.maximum(
        jnp.full((half, LANES), kept, jnp.int32).astype(jnp.float32), 1.0
    )
    for s in (z,) + others:
        relay_h(1, s)
    landed(h0.at[0:2], fin_sem.at[0])
    for s in range(n):
        rows_at = slice(s * n * SUB, (s + 1) * n * SUB)
        flat = h0[s, :, :, :, 0:hcols].astype(jnp.float32).reshape(n * SUB, hcols)
        hall[rows_at] = flat.astype(jnp.bfloat16)
        flag = h0[s, :, 1, :, hcols : hcols + LANES].astype(jnp.float32)
        for c in range(gcols // LANES):
            at = c * LANES
            sure = g0[s, :, 0, :, at : at + LANES].astype(jnp.float32)
            spare = g0[s, :, 1, :, at : at + LANES].astype(jnp.float32) * flag
            part = jnp.stack([sure, spare], axis=1).reshape(n * SUB, LANES)
            sides[at // side][rows_at, at % side : at % side + LANES] = part.astype(jnp.bfloat16)
    for s in (z,) + others:
        for j, k in enumerate((q, over)):
            view = hx.at[s, k]
            landed(view, hx_sem.at[j * n + s])
            send(view, view, fin_sem.at[2], beside)
    for s in range(n):
        landed(gx.at[s], gx_sem.at[s])
        rows_at = slice(n_both + s * n * half, n_both + (s + 1) * n * half)
        flag = h0[s, :, 1, :, hcols : hcols + LANES].astype(jnp.float32)
        for c in range(gcols // LANES):
            at = c * LANES
            part = gx[s, :, :, at : at + LANES].astype(jnp.float32) * flag
            part = part.reshape(n * half, LANES).astype(jnp.bfloat16)
            sides[at // side][rows_at, at % side : at % side + LANES] = part
    own_h(1).wait()
    landed(hall.at[pl.ds(n_first, 2 * n * SUB)], fin_sem.at[1])
    landed(hx.at[0:2], fin_sem.at[2])
    for s in range(n):
        rows_at = slice(n_both + s * n * half, n_both + (s + 1) * n * half)
        flat = hx[s].astype(jnp.float32).reshape(n * half, hcols)
        hall[rows_at] = flat.astype(jnp.bfloat16)
    for s in others:
        finish_g(1, s)
    step = made.shape[1]

    def leave(i, blocks, spun):
        at = pl.ds(pl.multiple_of(i * step, step), step)
        for b, block in enumerate(blocks):
            done[at, b * LANES : (b + 1) * LANES] = block
            tops[b, :, at] = spun[b : b + 1]

    forward_near(2)
    forward_far(2)
    block_grads(hall, g_left, factor_out[0:1], made, leave)
    for s in others:
        finish_g(2, s)
    landed(h0.at[0, 0:3], send_sem.at[2])
    landed(h0.at[0:2], send_sem.at[3])
    landed(h0.at[0], send_sem.at[4])
    landed(done.at[pl.ds(0, sent[0] // (2 * side))], send_sem.at[0])

    @pl.when(inner)
    def _():
        landed(done.at[pl.ds(0, sent[1] // (2 * side))], send_sem.at[1])


def grad_pairs(hidden, out_grad, counts, route_index, keep, capacity):
    replicas = lax.axis_size("dp")
    n = math.isqrt(replicas)
    hcols, gcols = hidden.shape[1] // n, out_grad.shape[1] // n
    half, side = SUB // 2, gcols // 2
    depth = 2 * n * n * SUB + n * n * half
    step = min(hcols, 512)
    kind = jnp.bfloat16
    vmem = pl.BlockSpec(memory_space=pltpu.VMEM)
    made = pl.pallas_call(
        functools.partial(spread_kernel, n, hidden.shape[0] - capacity),
        out_shape=[
            jax.ShapeDtypeStruct((depth, hcols), kind),
            jax.ShapeDtypeStruct((depth, side), kind),
            jax.ShapeDtypeStruct((depth, side), kind),
            jax.ShapeDtypeStruct((hcols, side), jnp.float32),
            jax.ShapeDtypeStruct((side // LANES, 1, hcols), jnp.float32),
            jax.ShapeDtypeStruct((half, LANES), jnp.float32),
        ],
        in_specs=[pl.BlockSpec(memory_space=pltpu.HBM)] * 5,
        out_specs=[vmem] * 6,
        scratch_shapes=[
            pltpu.SMEM(counts.shape, counts.dtype),
            pltpu.SMEM(keep.shape, keep.dtype),
            pltpu.VMEM(route_index.shape, route_index.dtype),
            pltpu.VMEM(hidden.shape, kind),
            pltpu.VMEM(out_grad.shape, kind),
            pltpu.VMEM((n, n, 2, half, hcols + LANES), kind),
            pltpu.VMEM((n, n, 2, half, gcols), kind),
            pltpu.VMEM((n, n, half, hcols), kind),
            pltpu.VMEM((n, n, half, gcols), kind),
            pltpu.VMEM((n, 2, half, hcols + LANES), kind),
            pltpu.VMEM((n, 2, half, gcols), kind),
            pltpu.VMEM((n, SUB, hcols), kind),
            pltpu.VMEM((2, n, SUB, side), kind),
            pltpu.VMEM((n, SUB, hcols), kind),
            pltpu.VMEM((n, SUB, gcols), kind),
            pltpu.VMEM((n, SUB, hcols), kind),
            pltpu.VMEM((n, SUB, gcols), kind),
            pltpu.VMEM((2, step, side), jnp.float32),
            pltpu.SemaphoreType.DMA((3 + 2 * n,)),
            pltpu.SemaphoreType.DMA((5,)),
            pltpu.SemaphoreType.DMA((4 * n,)),
            pltpu.SemaphoreType.DMA((3 * n * n,)),
            pltpu.SemaphoreType.DMA((2 * n,)),
            pltpu.SemaphoreType.DMA((n,)),
            pltpu.SemaphoreType.DMA((2,)),
            pltpu.SemaphoreType.DMA((3,)),
            pltpu.SemaphoreType.DMA((5,)),
            pltpu.SemaphoreType.REGULAR,
            pltpu.SemaphoreType.REGULAR,
        ],
        compiler_params=pltpu.CompilerParams(
            collective_id=0, has_side_effects=True, vmem_limit_bytes=36 << 20
        ),
        name="spread",
    )(*[pltpu.with_memory_space_constraint(x, pltpu.HBM) for x in (counts, keep, route_index, hidden, out_grad)])
    hall, _, g_right, done, tops, factor = made
    return pl.pallas_call(
        functools.partial(last_kernel, step),
        out_shape=[
            jax.ShapeDtypeStruct((hcols, gcols), jnp.float32),
            jax.ShapeDtypeStruct((gcols // LANES, 1, hcols), jnp.float32),
        ],
        in_specs=[vmem] * 5,
        out_specs=[pl.BlockSpec(memory_space=pltpu.HBM), vmem],
        scratch_shapes=[
            pltpu.VMEM((2, step, side), jnp.float32),
            pltpu.VMEM((hcols, side), jnp.float32),
            pltpu.SemaphoreType.DMA((hcols // step,)),
            pltpu.SemaphoreType.DMA((1,)),
        ],
        compiler_params=pltpu.CompilerParams(vmem_limit_bytes=20 << 20),
        name="last_side",
    )(hall, g_right, done, tops, factor)


def last_kernel(step, hall, g_right, done, tops, factor, out, scales, made, left, sems, done_sem):
    rows, side = done.shape
    first = pltpu.make_async_copy(done, out.at[:, 0:side], done_sem.at[0])
    first.start()
    scales[0 : tops.shape[0]] = tops[...]

    def away(i):
        at = pl.ds(pl.multiple_of(i * step, step), step)
        return pltpu.make_async_copy(left.at[at], out.at[at, side : 2 * side], sems.at[i])

    def leave(i, blocks, spun):
        at = pl.ds(pl.multiple_of(i * step, step), step)
        for b, block in enumerate(blocks):
            left[at, b * LANES : (b + 1) * LANES] = block
            scales[tops.shape[0] + b, :, at] = spun[b : b + 1]
        away(i).start()

    block_grads(hall, g_right, factor[0:1], made, leave)
    for i in range(rows // step):
        away(i).wait()
    first.wait()


def tile_kernel(pairs, keep, *refs):
    out, scales = refs[2 * pairs :]
    replicas = keep.shape[0]
    kept = keep[0]
    for i in range(1, replicas):
        kept = kept + keep[i]
    factor = jnp.float32(replicas) / jnp.maximum(
        jnp.full((1, LANES), kept, jnp.int32).astype(jnp.float32), 1.0
    )
    total = None
    for i in range(pairs):
        term = lax.dot_general(
            refs[2 * i][...],
            refs[2 * i + 1][...],
            (((0,), (0,)), ((), ())),
            preferred_element_type=jnp.float32,
        )
        total = term if total is None else total + term
    tops = []
    for b in range(out.shape[1] // LANES):
        block = total[:, b * LANES : (b + 1) * LANES] * factor
        top = jnp.max(jnp.abs(block), axis=1, keepdims=True)
        out[:, b * LANES : (b + 1) * LANES] = block * (1.0 / (top + 1e-6))
        tops.append(top)
    lane = lax.broadcasted_iota(jnp.int32, (out.shape[0], LANES), 1)
    packed = jnp.zeros((out.shape[0], LANES), jnp.float32)
    for b, top in enumerate(tops):
        packed = jnp.where(lane == b, top, packed)
    spun = packed.T
    for b in range(scales.shape[0]):
        scales[b] = spun[b : b + 1]


def tile_grad(pairs, keep):
    rows, cols = pairs[0][0].shape[1], pairs[0][1].shape[1]
    step = min(rows, 512)
    args, specs = [], []
    for h, g in pairs:
        args += [h, g]
        specs.append(pl.BlockSpec((h.shape[0], step), lambda i: (0, i)))
        specs.append(pl.BlockSpec((g.shape[0], cols), lambda i: (0, 0)))
    return pl.pallas_call(
        functools.partial(tile_kernel, len(pairs)),
        grid=(rows // step,),
        out_shape=[
            jax.ShapeDtypeStruct((rows, cols), jnp.float32),
            jax.ShapeDtypeStruct((cols // LANES, 1, rows), jnp.float32),
        ],
        in_specs=[pl.BlockSpec(memory_space=pltpu.SMEM)] + specs,
        out_specs=[
            pl.BlockSpec((step, cols), lambda i: (i, 0)),
            pl.BlockSpec((cols // LANES, 1, step), lambda i: (0, 0, i)),
        ],
        compiler_params=pltpu.CompilerParams(vmem_limit_bytes=32 << 20),
        name="tile_grad",
    )(keep, *args)


def on_device(hidden, out_grad, counts, route_index, keep):
    experts = lax.axis_size("expert")
    tok_rows = hidden.shape[0]
    capacity = max(tok_rows // 4, tok_rows // experts + 4)
    low = tok_rows - capacity
    paired = (
        experts == 2
        and lax.axis_size("dp") == 16
        and low == SUB - 4
        and capacity - low == SUB // 2
    )
    operands = (hidden, out_grad, counts, route_index, keep, capacity)
    if paired:
        normed, scales = grad_pairs(*operands)
    else:
        normed, scales = tile_grad(gather_general(*operands), keep)
    return (normed[None, None], jnp.transpose(scales[None], (0, 2, 3, 1)))


def solution(mesh):
    placed = (
        P(("dp", "expert"), None),
        P(("dp", "expert"), None),
        P(("dp", "expert"), None),
        P(("dp", "expert"), None),
        P(),
    )
    return jax.shard_map(
        on_device,
        mesh=mesh,
        in_specs=placed,
        out_specs=(P("expert", "dp", None, None), P("expert", "dp", None, None)),
        check_vma=False,
    )
```

```python
import functools
import math

import jax
import jax.numpy as jnp
from jax import lax
from jax.experimental import pallas as pl
from jax.experimental.pallas import tpu as pltpu
from jax.sharding import PartitionSpec as P

MESH = pl.DeviceIdType.MESH
LANES = 128
SUB = 16


def swapped(block, axis, bit):
    count = lax.axis_size(axis)
    route = []
    for low in range(count):
        high = low | 1 << bit
        if high != low and high < count:
            route += [(low, high), (high, low)]
    return lax.ppermute(block, axis, route)


def build_slots(rows_dev, counts_dev, perm_dev, capacity):
    ids = jnp.arange(counts_dev.shape[0], dtype=jnp.int32)
    before = ids[None, :] < ids[:, None]
    offsets = jnp.sum(jnp.where(before, counts_dev[None, :], 0), axis=1)
    slots = jnp.arange(capacity, dtype=jnp.int32)
    position = offsets[:, None] + slots[None, :]
    position = jnp.minimum(position, rows_dev.shape[0] - 1)
    live = slots[None, :] < counts_dev[:, None]
    local = perm_dev[position]
    picked = rows_dev[local]
    return jnp.where(live[:, :, None], picked, jnp.zeros_like(picked))


def join_pair(mine, partner, replica, bit):
    lower = replica >> bit & 1 == 0
    first = jnp.concatenate([mine, partner], axis=1)
    second = jnp.concatenate([partner, mine], axis=1)
    return jnp.where(lower, first, second)


def gather_general(hidden, out_grad, counts, route_index, keep, capacity):
    experts = lax.axis_size("expert")
    replicas = lax.axis_size("dp")
    side = math.isqrt(replicas)
    levels = side.bit_length() - 1
    replica = lax.axis_index("dp")
    hidden_units = hidden.shape[1]
    width = out_grad.shape[1]
    grad_rows = jnp.where(keep[replica] > 0, out_grad, jnp.zeros_like(out_grad))
    send_h = build_slots(hidden, counts[0], route_index[0], capacity)
    send_g = build_slots(grad_rows, counts[0], route_index[0], capacity)
    recv_h = lax.all_to_all(send_h, "expert", split_axis=0, concat_axis=0, tiled=True)
    recv_g = lax.all_to_all(send_g, "expert", split_axis=0, concat_axis=0, tiled=True)
    slot_count = experts * capacity
    tile_rows = hidden_units // side
    tile_cols = width // side
    sub_rows = slot_count // side
    piece_h = (
        recv_h.reshape(side, sub_rows, side, tile_rows)
        .transpose(2, 0, 1, 3)
        .reshape(replicas, sub_rows, tile_rows)
    )
    piece_g = (
        recv_g.reshape(side, sub_rows, side, tile_cols)
        .transpose(0, 2, 1, 3)
        .reshape(replicas, sub_rows, tile_cols)
    )
    all_h = lax.all_to_all(piece_h, "dp", split_axis=0, concat_axis=0, tiled=True)
    all_g = lax.all_to_all(piece_g, "dp", split_axis=0, concat_axis=0, tiled=True)
    for bit in range(levels):
        all_h = join_pair(all_h, swapped(all_h, "dp", bit), replica, bit)
    for bit in range(levels, 2 * levels):
        all_g = join_pair(all_g, swapped(all_g, "dp", bit), replica, bit)
    return [(all_h.reshape(-1, tile_rows), all_g.reshape(-1, tile_cols))]


def block_grads(h_ref, g_ref, factor, made, leave):
    step = made.shape[1]
    steps = h_ref.shape[1] // step

    def product(i, slot):
        made[slot] = lax.dot_general(
            h_ref[:, pl.ds(pl.multiple_of(i * step, step), step)],
            g_ref[...],
            (((0,), (0,)), ((), ())),
            preferred_element_type=jnp.float32,
        )

    def normalise(i, slot):
        lane = lax.broadcasted_iota(jnp.int32, (step, LANES), 1)
        packed = jnp.zeros((step, LANES), jnp.float32)
        blocks = []
        for b in range(g_ref.shape[1] // LANES):
            block = made[slot, :, b * LANES : (b + 1) * LANES] * factor
            top = jnp.max(jnp.abs(block), axis=1, keepdims=True)
            blocks.append(block * (1.0 / (top + 1e-6)))
            packed = jnp.where(lane == b, top, packed)
        leave(i, blocks, packed.T)

    product(0, 0)

    @pl.loop(0, steps // 2)
    def _(j):
        product(2 * j + 1, 1)
        normalise(2 * j, 0)
        product(jnp.minimum(2 * j + 2, steps - 1), 0)
        normalise(2 * j + 1, 1)


def spread_kernel(
    n, low, counts_in, keep_in, route_in, hidden_in, grad_in,
    hall, g_left, g_right, done, tops, factor_out,
    counts, keep, route, hidden, grad, h0, g0, hx, gx, h0s, g0s, hbs, gbs, hys, gys, hyr, gyr,
    made, in_sem, send_sem, h_sem, g_sem, hx_sem, gx_sem, y_sem, fin_sem, own_sem, two_sem, three_sem,
):
    here = lax.axis_index("dp")
    y = lax.axis_index("expert")
    z, q = here // n, here % n
    twin = q + 1 - 2 * (q % 2)
    over = (q + n // 2) % n
    far = (twin + n // 2) % n
    mate = z + 1 - 2 * (z % 2)
    jump = (z + 2) % n
    mirror = n - 1 - z
    others = (mate, jump, mirror)
    inner = jnp.logical_and(z >= 1, z + 1 < n)
    half = SUB // 2
    n_first = n * n * SUB
    n_both = 2 * n_first
    hcols, gcols = hall.shape[1], gx.shape[3]
    side = gcols // 2

    across = (here, 1 - y)
    beside = (z * n + twin, y)
    outward = (mate * n + q, y)
    inward = (mirror * n + q, y)

    def signal(sem, peer):
        pl.semaphore_signal(sem, inc=1, device_id=peer, device_id_type=MESH)

    barrier = pltpu.get_barrier_semaphore()
    for peer in (across, (z * n + over, y), (z * n + far, y), beside, outward):
        signal(barrier, peer)
    pl.when(inner)(lambda: signal(barrier, inward))

    moves = []
    for src, dst in ((counts_in, counts), (keep_in, keep), (route_in, route)):
        moves.append(pltpu.make_async_copy(src, dst, in_sem.at[len(moves)]))
    for src, dst in ((grad_in, grad), (hidden_in, hidden)):
        moves.append(pltpu.make_async_copy(src, dst, in_sem.at[len(moves)]))
    for move in moves:
        move.start()

    for move in moves[:3]:
        move.wait()
    due = moves[3:]
    rows = hidden.shape[0]
    total = 3 * SUB
    row = lax.broadcasted_iota(jnp.int32, (total, rows), 0)
    pos = lax.broadcasted_iota(jnp.int32, (total, rows), 1)
    first, second = counts[0, 0], counts[0, 1]
    hot = jnp.where(first > second, 0, 1)
    in_spare = jnp.logical_and(row >= half, row < SUB)
    in_send = row >= 2 * SUB
    expert = jnp.where(in_spare, hot, jnp.where(in_send, 1 - y, y))
    slot = jnp.where(row < half, row, row - half + low)
    slot = jnp.where(row >= SUB, row - SUB - low + half, slot)
    slot = jnp.where(in_send, row - 2 * SUB, slot)
    low_slot = jnp.where(in_send, 0, jnp.where(row < SUB, 0, half))
    high_slot = jnp.where(in_send, low, jnp.where(row < SUB, rows, low))
    valid = jnp.logical_and(slot >= low_slot, slot < high_slot)
    start = jnp.where(expert == 0, 0, first)
    count = jnp.where(expert == 0, first, second)
    take = jnp.logical_and(valid, jnp.logical_and(slot < count, pos == start + slot))
    take = jnp.where(take, 1.0, 0.0).astype(jnp.bfloat16)
    local = lax.broadcasted_iota(jnp.int32, (rows, rows), 0)
    perm = jnp.where(local == route[...], 1.0, 0.0).astype(jnp.bfloat16)
    pick = lax.dot_general(
        take, perm, (((1,), (1,)), ((), ())), preferred_element_type=jnp.float32
    )
    pick_h = pick.astype(jnp.bfloat16)
    pick_g = jnp.where(keep[here] > 0, pick, 0.0).astype(jnp.bfloat16)

    def pick_rows(pick_x, src, x0s, xys):
        cols = xys.shape[2]
        due.pop(0).wait()
        for part in range(n):
            got = jnp.dot(
                pick_x,
                src[:, part * cols : (part + 1) * cols],
                preferred_element_type=jnp.float32,
            )
            x0s[part, 0, :, 0:cols] = got[:half].astype(jnp.bfloat16)
            x0s[part, 1, :, 0:cols] = got[half:SUB].astype(jnp.bfloat16)
            xys[part] = got[2 * SUB :].astype(jnp.bfloat16)
            rest = got[SUB : 2 * SUB].astype(jnp.bfloat16)
            if x0s is h0s:
                hbs[part] = rest
            else:
                gbs[0, part] = rest[:, :side]
                gbs[1, part] = rest[:, side:]

    mine = jnp.ones((half, LANES), jnp.float32) * jnp.where(hot == y, 1.0, 0.0)
    for part in range(n):
        h0s[part, 0, :, hcols : hcols + LANES] = jnp.ones((half, LANES), jnp.bfloat16)
        h0s[part, 1, :, hcols : hcols + LANES] = mine.astype(jnp.bfloat16)
    pick_rows(pick_g, grad, g0s, gys)
    enter = 5 + jnp.minimum(z, 1) * jnp.minimum(n - 1 - z, 1)
    pl.semaphore_wait(barrier, enter)

    sent = [0] * 5

    def send(src, dst, sem, peer, when=None, group=0, again=False):
        if not again:
            sent[group] += math.prod(src.shape)
        copy = pltpu.make_async_remote_copy(
            src_ref=src,
            dst_ref=dst,
            send_sem=send_sem.at[group],
            recv_sem=sem,
            device_id=peer,
            device_id_type=MESH,
        )
        if when is None:
            copy.start()
        else:
            pl.when(when)(copy.start)

    def landed(view, sem):
        pltpu.make_async_copy(view, view, sem).wait()

    sides = (g_left, g_right)

    def h_view(b, s, k):
        if b == 0:
            return h0.at[s, k]
        return hall.at[pl.ds(pl.multiple_of(n_first + (s * n + k) * SUB, SUB), SUB)]

    def g_view(b, s, k):
        if b == 0:
            return g0.at[s, k]
        at = pl.multiple_of(n_first + (s * n + k) * SUB, SUB)
        return sides[b - 1].at[pl.ds(at, SUB)]

    h_own = lambda b, k: (h0s, hbs)[b].at[k]
    g_own = lambda b, k: g0s.at[k] if b == 0 else gbs.at[b - 1, k]
    h_at = lambda b, s: h_sem.at[2 * n * b + s]
    h_over = lambda b, s: h_sem.at[2 * n * b + n + s]
    g_at = lambda b, s, k: g_sem.at[(b * n + s) * n + k]

    def own_h(b):
        return pltpu.make_async_copy(h_own(b, z), h_view(b, z, q), own_sem.at[b])

    def own_g(b):
        return pltpu.make_async_copy(g_own(b, q), g_view(b, z, q), own_sem.at[2 + b])

    def start_g(b):
        for to in (over, far, twin):
            send(g_own(b, to), g_view(b, z, q), g_at(b, z, q), (z * n + to, y))
        own_g(b).start()

    def both_ways(view, sem):
        send(view, view, sem, outward)
        send(view, view, sem, inward, inner, 1)

    def first_g():
        send(g_own(0, q), g_view(0, z, q), g_at(0, z, q), outward)
        send(g_own(0, q), g_view(0, z, q), g_at(0, z, q), inward, inner, 1)

    def plane_g(b):
        if b > 0:
            own_g(b).wait()
            both_ways(g_view(b, z, q), g_at(b, z, q))
        for k in (twin, over, far):
            landed(g_view(b, z, k), g_at(b, z, k))
            both_ways(g_view(b, z, k), g_at(b, z, k))

    def start_h(b, s, when=None, again=False):
        to = (s * n + q, y)
        send(h_own(b, s), h_view(b, z, q), h_at(b, z), to, when, 0 if b else 2, again)

    def own_fan(b):
        group = 0 if b else 3
        send(h_own(b, z), h_view(b, z, q), h_over(b, z), (z * n + over, y), None, group)
        send(h_own(b, z), h_view(b, z, q), fin_sem.at[b], beside, None, group)
        own_h(b).start()

    def forward_g(b, s, peer):
        for k in (q, twin, over, far):
            view, sem = g_view(b, s, k), g_at(b, s, k)
            pl.when(inner)(functools.partial(landed, view, sem))
            send(view, view, sem, peer, inner, 1)

    def forward_near(b):
        forward_g(b, mate, inward)
        forward_g(b, mirror, outward)

    def forward_far(b):
        forward_g(b, jump, outward)

    def finish_g(b, s):
        for k in (q, twin, over, far):
            pl.when(jnp.logical_not(inner))(
                functools.partial(landed, g_view(b, s, k), g_at(b, s, k))
            )

    def fan_h(b, s):
        view, group = h_view(b, s, q), 0 if b else 3
        landed(view, h_at(b, s))
        send(view, view, h_over(b, s), (z * n + over, y), None, group)
        send(view, view, fin_sem.at[b], beside, None, group)

    def relay_h(b, s):
        view = h_view(b, s, over)
        landed(view, h_over(b, s))
        send(view, view, fin_sem.at[b], beside, None, 0 if b else 4)

    def cross_h(s):
        for k in (q, over):
            send(h0.at[s, k, 1, :, 0:hcols], hx.at[s, k], hx_sem.at[s], across)

    def cross_g(s):
        send(g0.at[s, :, 1, :, 0:gcols], gx.at[s], gx_sem.at[s], across)

    start_g(0)
    first_g()
    send(gys, gyr, y_sem.at[0], across)

    @pl.when(inner)
    def _():
        signal(two_sem, outward)
        signal(two_sem, inward)

    pick_rows(pick_h, hidden, h0s, hys)
    start_h(0, mate)
    start_h(0, mirror, inner)
    own_fan(0)
    send(hys, hyr, y_sem.at[1], across)
    plane_g(0)
    pl.semaphore_wait(two_sem, 1)
    pl.when(inner)(lambda: signal(three_sem, outward))
    start_h(0, jump)
    fan_h(0, mate)
    forward_near(0)
    pl.when(jnp.logical_not(inner))(lambda: pl.semaphore_wait(three_sem, 1))
    start_h(0, mirror, jnp.logical_not(inner), True)
    landed(gyr, y_sem.at[0])
    for b in (0, 1):
        gbs[b] = gbs[b] + gyr[:, :, b * side : (b + 1) * side]
        start_g(1 + b)
    fan_h(0, jump)
    fan_h(0, mirror)
    for s in (z,) + others:
        relay_h(0, s)
    landed(hyr, y_sem.at[1])
    hbs[...] = hbs[...] + hyr[...]
    for s in others:
        start_h(1, s)
    own_fan(1)
    own_h(0).wait()
    own_g(0).wait()
    cross_h(z)
    cross_g(z)
    finish_g(0, mate)
    cross_h(mate)
    cross_g(mate)
    forward_far(0)
    plane_g(1)
    for s in (jump, mirror):
        cross_h(s)
        finish_g(0, s)
        cross_g(s)
    fan_h(1, mate)
    forward_near(1)
    plane_g(2)
    fan_h(1, jump)
    fan_h(1, mirror)
    forward_far(1)
    forward_g(2, mate, inward)
    kept = keep[0]
    for i in range(1, n * n):
        kept = kept + keep[i]
    factor_out[...] = jnp.float32(n * n) / jnp.maximum(
        jnp.full((half, LANES), kept, jnp.int32).astype(jnp.float32), 1.0
    )
    for s in (z,) + others:
        relay_h(1, s)
    landed(h0.at[0:2], fin_sem.at[0])
    for s in range(n):
        rows_at = slice(s * n * SUB, (s + 1) * n * SUB)
        flat = h0[s, :, :, :, 0:hcols].astype(jnp.float32).reshape(n * SUB, hcols)
        hall[rows_at] = flat.astype(jnp.bfloat16)
        flag = h0[s, :, 1, :, hcols : hcols + LANES].astype(jnp.float32)
        for c in range(gcols // LANES):
            at = c * LANES
            sure = g0[s, :, 0, :, at : at + LANES].astype(jnp.float32)
            spare = g0[s, :, 1, :, at : at + LANES].astype(jnp.float32) * flag
            part = jnp.stack([sure, spare], axis=1).reshape(n * SUB, LANES)
            sides[at // side][rows_at, at % side : at % side + LANES] = part.astype(jnp.bfloat16)
    for s in (z,) + others:
        landed(hx.at[s, 0:2], hx_sem.at[s])
        for k in (q, over):
            send(hx.at[s, k], hx.at[s, k], fin_sem.at[2], beside)
    for s in range(n):
        landed(gx.at[s], gx_sem.at[s])
        rows_at = slice(n_both + s * n * half, n_both + (s + 1) * n * half)
        flag = h0[s, :, 1, :, hcols : hcols + LANES].astype(jnp.float32)
        for c in range(gcols // LANES):
            at = c * LANES
            part = gx[s, :, :, at : at + LANES].astype(jnp.float32) * flag
            part = part.reshape(n * half, LANES).astype(jnp.bfloat16)
            sides[at // side][rows_at, at % side : at % side + LANES] = part
    own_h(1).wait()
    landed(hall.at[pl.ds(n_first, 2 * n * SUB)], fin_sem.at[1])
    landed(hx.at[0:2], fin_sem.at[2])
    for s in range(n):
        rows_at = slice(n_both + s * n * half, n_both + (s + 1) * n * half)
        flat = hx[s].astype(jnp.float32).reshape(n * half, hcols)
        hall[rows_at] = flat.astype(jnp.bfloat16)
    for s in others:
        finish_g(1, s)
    step = made.shape[1]

    def leave(i, blocks, spun):
        at = pl.ds(pl.multiple_of(i * step, step), step)
        for b, block in enumerate(blocks):
            done[at, b * LANES : (b + 1) * LANES] = block
            tops[b, :, at] = spun[b : b + 1]

    forward_g(2, mirror, outward)
    forward_far(2)
    block_grads(hall, g_left, factor_out[0:1], made, leave)
    for s in others:
        finish_g(2, s)
    landed(h0.at[0, 0:3], send_sem.at[2])
    landed(h0.at[0:2], send_sem.at[3])
    landed(h0.at[0], send_sem.at[4])
    landed(done.at[pl.ds(0, sent[0] // (2 * side))], send_sem.at[0])

    @pl.when(inner)
    def _():
        landed(done.at[pl.ds(0, sent[1] // (2 * side))], send_sem.at[1])


def grad_pairs(hidden, out_grad, counts, route_index, keep, capacity):
    replicas = lax.axis_size("dp")
    n = math.isqrt(replicas)
    hcols, gcols = hidden.shape[1] // n, out_grad.shape[1] // n
    half, side = SUB // 2, gcols // 2
    depth = 2 * n * n * SUB + n * n * half
    step = min(hcols, 512)
    kind = jnp.bfloat16
    vmem = pl.BlockSpec(memory_space=pltpu.VMEM)
    made = pl.pallas_call(
        functools.partial(spread_kernel, n, hidden.shape[0] - capacity),
        out_shape=[
            jax.ShapeDtypeStruct((depth, hcols), kind),
            jax.ShapeDtypeStruct((depth, side), kind),
            jax.ShapeDtypeStruct((depth, side), kind),
            jax.ShapeDtypeStruct((hcols, side), jnp.float32),
            jax.ShapeDtypeStruct((side // LANES, 1, hcols), jnp.float32),
            jax.ShapeDtypeStruct((half, LANES), jnp.float32),
        ],
        in_specs=[pl.BlockSpec(memory_space=pltpu.HBM)] * 5,
        out_specs=[vmem] * 6,
        scratch_shapes=[
            pltpu.SMEM(counts.shape, counts.dtype),
            pltpu.SMEM(keep.shape, keep.dtype),
            pltpu.VMEM(route_index.shape, route_index.dtype),
            pltpu.VMEM(hidden.shape, kind),
            pltpu.VMEM(out_grad.shape, kind),
            pltpu.VMEM((n, n, 2, half, hcols + LANES), kind),
            pltpu.VMEM((n, n, 2, half, gcols), kind),
            pltpu.VMEM((n, n, half, hcols), kind),
            pltpu.VMEM((n, n, half, gcols), kind),
            pltpu.VMEM((n, 2, half, hcols + LANES), kind),
            pltpu.VMEM((n, 2, half, gcols), kind),
            pltpu.VMEM((n, SUB, hcols), kind),
            pltpu.VMEM((2, n, SUB, side), kind),
            pltpu.VMEM((n, SUB, hcols), kind),
            pltpu.VMEM((n, SUB, gcols), kind),
            pltpu.VMEM((n, SUB, hcols), kind),
            pltpu.VMEM((n, SUB, gcols), kind),
            pltpu.VMEM((2, step, side), jnp.float32),
            pltpu.SemaphoreType.DMA((5,)),
            pltpu.SemaphoreType.DMA((5,)),
            pltpu.SemaphoreType.DMA((4 * n,)),
            pltpu.SemaphoreType.DMA((3 * n * n,)),
            pltpu.SemaphoreType.DMA((n,)),
            pltpu.SemaphoreType.DMA((n,)),
            pltpu.SemaphoreType.DMA((2,)),
            pltpu.SemaphoreType.DMA((3,)),
            pltpu.SemaphoreType.DMA((5,)),
            pltpu.SemaphoreType.REGULAR,
            pltpu.SemaphoreType.REGULAR,
        ],
        compiler_params=pltpu.CompilerParams(
            collective_id=0, has_side_effects=True, vmem_limit_bytes=36 << 20
        ),
        name="spread",
    )(*[pltpu.with_memory_space_constraint(x, pltpu.HBM) for x in (counts, keep, route_index, hidden, out_grad)])
    hall, _, g_right, done, tops, factor = made
    return pl.pallas_call(
        functools.partial(last_kernel, step),
        out_shape=[
            jax.ShapeDtypeStruct((hcols, gcols), jnp.float32),
            jax.ShapeDtypeStruct((gcols // LANES, 1, hcols), jnp.float32),
        ],
        in_specs=[vmem] * 5,
        out_specs=[pl.BlockSpec(memory_space=pltpu.HBM), vmem],
        scratch_shapes=[
            pltpu.VMEM((2, step, side), jnp.float32),
            pltpu.VMEM((hcols, side), jnp.float32),
            pltpu.SemaphoreType.DMA((hcols // step,)),
            pltpu.SemaphoreType.DMA((1,)),
        ],
        compiler_params=pltpu.CompilerParams(vmem_limit_bytes=20 << 20),
        name="last_side",
    )(hall, g_right, done, tops, factor)


def last_kernel(step, hall, g_right, done, tops, factor, out, scales, made, left, sems, done_sem):
    rows, side = done.shape
    first = pltpu.make_async_copy(done, out.at[:, 0:side], done_sem.at[0])
    first.start()
    scales[0 : tops.shape[0]] = tops[...]

    def away(i):
        at = pl.ds(pl.multiple_of(i * step, step), step)
        return pltpu.make_async_copy(left.at[at], out.at[at, side : 2 * side], sems.at[i])

    def leave(i, blocks, spun):
        at = pl.ds(pl.multiple_of(i * step, step), step)
        for b, block in enumerate(blocks):
            left[at, b * LANES : (b + 1) * LANES] = block
            scales[tops.shape[0] + b, :, at] = spun[b : b + 1]
        away(i).start()

    block_grads(hall, g_right, factor[0:1], made, leave)
    for i in range(rows // step):
        away(i).wait()
    first.wait()


def tile_kernel(pairs, keep, *refs):
    out, scales = refs[2 * pairs :]
    replicas = keep.shape[0]
    kept = keep[0]
    for i in range(1, replicas):
        kept = kept + keep[i]
    factor = jnp.float32(replicas) / jnp.maximum(
        jnp.full((1, LANES), kept, jnp.int32).astype(jnp.float32), 1.0
    )
    total = None
    for i in range(pairs):
        term = lax.dot_general(
            refs[2 * i][...],
            refs[2 * i + 1][...],
            (((0,), (0,)), ((), ())),
            preferred_element_type=jnp.float32,
        )
        total = term if total is None else total + term
    tops = []
    for b in range(out.shape[1] // LANES):
        block = total[:, b * LANES : (b + 1) * LANES] * factor
        top = jnp.max(jnp.abs(block), axis=1, keepdims=True)
        out[:, b * LANES : (b + 1) * LANES] = block * (1.0 / (top + 1e-6))
        tops.append(top)
    lane = lax.broadcasted_iota(jnp.int32, (out.shape[0], LANES), 1)
    packed = jnp.zeros((out.shape[0], LANES), jnp.float32)
    for b, top in enumerate(tops):
        packed = jnp.where(lane == b, top, packed)
    spun = packed.T
    for b in range(scales.shape[0]):
        scales[b] = spun[b : b + 1]


def tile_grad(pairs, keep):
    rows, cols = pairs[0][0].shape[1], pairs[0][1].shape[1]
    step = min(rows, 512)
    args, specs = [], []
    for h, g in pairs:
        args += [h, g]
        specs.append(pl.BlockSpec((h.shape[0], step), lambda i: (0, i)))
        specs.append(pl.BlockSpec((g.shape[0], cols), lambda i: (0, 0)))
    return pl.pallas_call(
        functools.partial(tile_kernel, len(pairs)),
        grid=(rows // step,),
        out_shape=[
            jax.ShapeDtypeStruct((rows, cols), jnp.float32),
            jax.ShapeDtypeStruct((cols // LANES, 1, rows), jnp.float32),
        ],
        in_specs=[pl.BlockSpec(memory_space=pltpu.SMEM)] + specs,
        out_specs=[
            pl.BlockSpec((step, cols), lambda i: (i, 0)),
            pl.BlockSpec((cols // LANES, 1, step), lambda i: (0, 0, i)),
        ],
        compiler_params=pltpu.CompilerParams(vmem_limit_bytes=32 << 20),
        name="tile_grad",
    )(keep, *args)


def on_device(hidden, out_grad, counts, route_index, keep):
    experts = lax.axis_size("expert")
    tok_rows = hidden.shape[0]
    capacity = max(tok_rows // 4, tok_rows // experts + 4)
    low = tok_rows - capacity
    paired = (
        experts == 2
        and lax.axis_size("dp") == 16
        and low == SUB - 4
        and capacity - low == SUB // 2
    )
    operands = (hidden, out_grad, counts, route_index, keep, capacity)
    if paired:
        normed, scales = grad_pairs(*operands)
    else:
        normed, scales = tile_grad(gather_general(*operands), keep)
    return (normed[None, None], jnp.transpose(scales[None], (0, 2, 3, 1)))


def solution(mesh):
    placed = (
        P(("dp", "expert"), None),
        P(("dp", "expert"), None),
        P(("dp", "expert"), None),
        P(("dp", "expert"), None),
        P(),
    )
    return jax.shard_map(
        on_device,
        mesh=mesh,
        in_specs=placed,
        out_specs=(P("expert", "dp", None, None), P("expert", "dp", None, None)),
        check_vma=False,
    )
```

```python
import functools
import math

import jax
import jax.numpy as jnp
from jax import lax
from jax.experimental import pallas as pl
from jax.experimental.pallas import tpu as pltpu
from jax.sharding import PartitionSpec as P

MESH = pl.DeviceIdType.MESH
LANES = 128
SUB = 16


def swapped(block, axis, bit):
    count = lax.axis_size(axis)
    route = []
    for low in range(count):
        high = low | 1 << bit
        if high != low and high < count:
            route += [(low, high), (high, low)]
    return lax.ppermute(block, axis, route)


def build_slots(rows_dev, counts_dev, perm_dev, capacity):
    ids = jnp.arange(counts_dev.shape[0], dtype=jnp.int32)
    before = ids[None, :] < ids[:, None]
    offsets = jnp.sum(jnp.where(before, counts_dev[None, :], 0), axis=1)
    slots = jnp.arange(capacity, dtype=jnp.int32)
    position = offsets[:, None] + slots[None, :]
    position = jnp.minimum(position, rows_dev.shape[0] - 1)
    live = slots[None, :] < counts_dev[:, None]
    local = perm_dev[position]
    picked = rows_dev[local]
    return jnp.where(live[:, :, None], picked, jnp.zeros_like(picked))


def join_pair(mine, partner, replica, bit):
    lower = replica >> bit & 1 == 0
    first = jnp.concatenate([mine, partner], axis=1)
    second = jnp.concatenate([partner, mine], axis=1)
    return jnp.where(lower, first, second)


def gather_general(hidden, out_grad, counts, route_index, keep, capacity):
    experts = lax.axis_size("expert")
    replicas = lax.axis_size("dp")
    side = math.isqrt(replicas)
    levels = side.bit_length() - 1
    replica = lax.axis_index("dp")
    hidden_units = hidden.shape[1]
    width = out_grad.shape[1]
    grad_rows = jnp.where(keep[replica] > 0, out_grad, jnp.zeros_like(out_grad))
    send_h = build_slots(hidden, counts[0], route_index[0], capacity)
    send_g = build_slots(grad_rows, counts[0], route_index[0], capacity)
    recv_h = lax.all_to_all(send_h, "expert", split_axis=0, concat_axis=0, tiled=True)
    recv_g = lax.all_to_all(send_g, "expert", split_axis=0, concat_axis=0, tiled=True)
    slot_count = experts * capacity
    tile_rows = hidden_units // side
    tile_cols = width // side
    sub_rows = slot_count // side
    piece_h = (
        recv_h.reshape(side, sub_rows, side, tile_rows)
        .transpose(2, 0, 1, 3)
        .reshape(replicas, sub_rows, tile_rows)
    )
    piece_g = (
        recv_g.reshape(side, sub_rows, side, tile_cols)
        .transpose(0, 2, 1, 3)
        .reshape(replicas, sub_rows, tile_cols)
    )
    all_h = lax.all_to_all(piece_h, "dp", split_axis=0, concat_axis=0, tiled=True)
    all_g = lax.all_to_all(piece_g, "dp", split_axis=0, concat_axis=0, tiled=True)
    for bit in range(levels):
        all_h = join_pair(all_h, swapped(all_h, "dp", bit), replica, bit)
    for bit in range(levels, 2 * levels):
        all_g = join_pair(all_g, swapped(all_g, "dp", bit), replica, bit)
    return [(all_h.reshape(-1, tile_rows), all_g.reshape(-1, tile_cols))]


def block_grads(h_ref, g_ref, factor, made, leave):
    step = made.shape[1]
    steps = h_ref.shape[1] // step

    def product(i, slot):
        made[slot] = lax.dot_general(
            h_ref[:, pl.ds(pl.multiple_of(i * step, step), step)],
            g_ref[...],
            (((0,), (0,)), ((), ())),
            preferred_element_type=jnp.float32,
        )

    def normalise(i, slot):
        lane = lax.broadcasted_iota(jnp.int32, (step, LANES), 1)
        packed = jnp.zeros((step, LANES), jnp.float32)
        blocks = []
        for b in range(g_ref.shape[1] // LANES):
            block = made[slot, :, b * LANES : (b + 1) * LANES] * factor
            top = jnp.max(jnp.abs(block), axis=1, keepdims=True)
            blocks.append(block * (1.0 / (top + 1e-6)))
            packed = jnp.where(lane == b, top, packed)
        leave(i, blocks, packed.T)

    product(0, 0)

    @pl.loop(0, steps // 2)
    def _(j):
        product(2 * j + 1, 1)
        normalise(2 * j, 0)
        product(jnp.minimum(2 * j + 2, steps - 1), 0)
        normalise(2 * j + 1, 1)


def spread_kernel(
    n, low, counts_in, keep_in, route_in, hidden_in, grad_in,
    hall, g_left, g_right, done, tops, factor_out,
    counts, keep, route, hidden, grad, h0, g0, hx, gx, h0s, g0s, hbs, gbs, hys, gys, hyr, gyr,
    made, in_sem, send_sem, h_sem, g_sem, hx_sem, gx_sem, y_sem, fin_sem, own_sem, two_sem, three_sem,
):
    here = lax.axis_index("dp")
    y = lax.axis_index("expert")
    z, q = here // n, here % n
    twin = q + 1 - 2 * (q % 2)
    over = (q + n // 2) % n
    far = (twin + n // 2) % n
    mate = z + 1 - 2 * (z % 2)
    jump = (z + 2) % n
    mirror = n - 1 - z
    others = (mate, jump, mirror)
    inner = jnp.logical_and(z >= 1, z + 1 < n)
    half = SUB // 2
    n_first = n * n * SUB
    n_both = 2 * n_first
    hcols, gcols = hall.shape[1], gx.shape[3]
    side = gcols // 2

    across = (here, 1 - y)
    beside = (z * n + twin, y)
    outward = (mate * n + q, y)
    inward = (mirror * n + q, y)

    def signal(sem, peer):
        pl.semaphore_signal(sem, inc=1, device_id=peer, device_id_type=MESH)

    barrier = pltpu.get_barrier_semaphore()
    for peer in (across, (z * n + over, y), (z * n + far, y), beside, outward):
        signal(barrier, peer)
    pl.when(inner)(lambda: signal(barrier, inward))

    moves = []
    for src, dst in ((counts_in, counts), (keep_in, keep), (route_in, route)):
        moves.append(pltpu.make_async_copy(src, dst, in_sem.at[len(moves)]))
    for src, dst in ((grad_in, grad), (hidden_in, hidden)):
        cols = src.shape[1] // n
        for part in range(n):
            cut = (slice(None), pl.ds(part * cols, cols))
            moves.append(pltpu.make_async_copy(src.at[cut], dst.at[cut], in_sem.at[len(moves)]))
    for move in moves:
        move.start()

    for move in moves[:3]:
        move.wait()
    due = moves[3:]
    rows = hidden.shape[0]
    total = 3 * SUB
    row = lax.broadcasted_iota(jnp.int32, (total, rows), 0)
    pos = lax.broadcasted_iota(jnp.int32, (total, rows), 1)
    first, second = counts[0, 0], counts[0, 1]
    hot = jnp.where(first > second, 0, 1)
    in_spare = jnp.logical_and(row >= half, row < SUB)
    in_send = row >= 2 * SUB
    expert = jnp.where(in_spare, hot, jnp.where(in_send, 1 - y, y))
    slot = jnp.where(row < half, row, row - half + low)
    slot = jnp.where(row >= SUB, row - SUB - low + half, slot)
    slot = jnp.where(in_send, row - 2 * SUB, slot)
    low_slot = jnp.where(in_send, 0, jnp.where(row < SUB, 0, half))
    high_slot = jnp.where(in_send, low, jnp.where(row < SUB, rows, low))
    valid = jnp.logical_and(slot >= low_slot, slot < high_slot)
    start = jnp.where(expert == 0, 0, first)
    count = jnp.where(expert == 0, first, second)
    take = jnp.logical_and(valid, jnp.logical_and(slot < count, pos == start + slot))
    take = jnp.where(take, 1.0, 0.0).astype(jnp.bfloat16)
    local = lax.broadcasted_iota(jnp.int32, (rows, rows), 0)
    perm = jnp.where(local == route[...], 1.0, 0.0).astype(jnp.bfloat16)
    pick = lax.dot_general(
        take, perm, (((1,), (1,)), ((), ())), preferred_element_type=jnp.float32
    )
    pick_h = pick.astype(jnp.bfloat16)
    pick_g = jnp.where(keep[here] > 0, pick, 0.0).astype(jnp.bfloat16)

    def pick_rows(pick_x, src, x0s, xys):
        cols = xys.shape[2]
        for part in range(n):
            due.pop(0).wait()
            got = jnp.dot(
                pick_x,
                src[:, part * cols : (part + 1) * cols],
                preferred_element_type=jnp.float32,
            )
            x0s[part, 0, :, 0:cols] = got[:half].astype(jnp.bfloat16)
            x0s[part, 1, :, 0:cols] = got[half:SUB].astype(jnp.bfloat16)
            xys[part] = got[2 * SUB :].astype(jnp.bfloat16)
            rest = got[SUB : 2 * SUB].astype(jnp.bfloat16)
            if x0s is h0s:
                hbs[part] = rest
            else:
                gbs[0, part] = rest[:, :side]
                gbs[1, part] = rest[:, side:]

    mine = jnp.ones((half, LANES), jnp.float32) * jnp.where(hot == y, 1.0, 0.0)
    for part in range(n):
        h0s[part, 0, :, hcols : hcols + LANES] = jnp.ones((half, LANES), jnp.bfloat16)
        h0s[part, 1, :, hcols : hcols + LANES] = mine.astype(jnp.bfloat16)
    pick_rows(pick_g, grad, g0s, gys)
    enter = 5 + jnp.minimum(z, 1) * jnp.minimum(n - 1 - z, 1)
    pl.semaphore_wait(barrier, enter)

    sent = [0] * 5

    def send(src, dst, sem, peer, when=None, group=0, again=False):
        if not again:
            sent[group] += math.prod(src.shape)
        copy = pltpu.make_async_remote_copy(
            src_ref=src,
            dst_ref=dst,
            send_sem=send_sem.at[group],
            recv_sem=sem,
            device_id=peer,
            device_id_type=MESH,
        )
        if when is None:
            copy.start()
        else:
            pl.when(when)(copy.start)

    def landed(view, sem):
        pltpu.make_async_copy(view, view, sem).wait()

    sides = (g_left, g_right)

    def h_view(b, s, k):
        if b == 0:
            return h0.at[s, k]
        return hall.at[pl.ds(pl.multiple_of(n_first + (s * n + k) * SUB, SUB), SUB)]

    def g_view(b, s, k, chunks=1):
        if b == 0:
            return g0.at[s, k]
        at = pl.multiple_of(n_first + (s * n + k) * SUB, SUB)
        return sides[b - 1].at[pl.ds(at, chunks * SUB)]

    h_own = lambda b, k: (h0s, hbs)[b].at[k]
    g_own = lambda b, k: g0s.at[k] if b == 0 else gbs.at[b - 1, k]
    h_at = lambda b, s: h_sem.at[2 * n * b + s]
    h_over = lambda b, s: h_sem.at[2 * n * b + n + s]
    g_at = lambda b, s, k: g_sem.at[(b * n + s) * n + k]
    chunks = lambda b: [(k, 1) for k in (q, twin, over, far)] if b == 0 else [(q - q % 2, 2), (over - over % 2, 2)]

    def own_h(b):
        return pltpu.make_async_copy(h_own(b, z), h_view(b, z, q), own_sem.at[b])

    def own_g(b):
        return pltpu.make_async_copy(g_own(b, q), g_view(b, z, q), own_sem.at[2 + b])

    def start_g(b):
        for to in (over, far, twin):
            send(g_own(b, to), g_view(b, z, q), g_at(b, z, q), (z * n + to, y))
        own_g(b).start()

    def both_ways(view, sem):
        send(view, view, sem, outward)
        send(view, view, sem, inward, inner, 1)

    def first_g():
        send(g_own(0, q), g_view(0, z, q), g_at(0, z, q), outward)
        send(g_own(0, q), g_view(0, z, q), g_at(0, z, q), inward, inner, 1)

    def plane_g(b):
        if b == 0:
            for k in (twin, over, far):
                landed(g_view(b, z, k), g_at(b, z, k))
                both_ways(g_view(b, z, k), g_at(b, z, k))
            return
        own_g(b).wait()
        for pair in ((twin,), (over, far)):
            for k in pair:
                landed(g_view(b, z, k), g_at(b, z, k))
            k = pair[0] - pair[0] % 2
            both_ways(g_view(b, z, k, 2), g_at(b, z, k))

    def start_h(b, s, when=None, again=False):
        to = (s * n + q, y)
        send(h_own(b, s), h_view(b, z, q), h_at(b, z), to, when, 0 if b else 2, again)

    def own_fan(b):
        group = 0 if b else 3
        send(h_own(b, z), h_view(b, z, q), h_over(b, z), (z * n + over, y), None, group)
        send(h_own(b, z), h_view(b, z, q), fin_sem.at[b], beside, None, group)
        own_h(b).start()

    def forward_g(b, s, peer):
        for k, count in chunks(b):
            view, sem = g_view(b, s, k, count), g_at(b, s, k)
            pl.when(inner)(functools.partial(landed, view, sem))
            send(view, view, sem, peer, inner, 1)

    def forward_near(b):
        forward_g(b, mate, inward)
        forward_g(b, mirror, outward)

    def forward_far(b):
        forward_g(b, jump, outward)

    def finish_g(b, s):
        for k, count in chunks(b):
            pl.when(jnp.logical_not(inner))(
                functools.partial(landed, g_view(b, s, k, count), g_at(b, s, k))
            )

    def fan_h(b, s):
        view, group = h_view(b, s, q), 0 if b else 3
        landed(view, h_at(b, s))
        send(view, view, h_over(b, s), (z * n + over, y), None, group)
        send(view, view, fin_sem.at[b], beside, None, group)

    def relay_h(b, s):
        view = h_view(b, s, over)
        landed(view, h_over(b, s))
        send(view, view, fin_sem.at[b], beside, None, 0 if b else 4)

    def cross_h(s):
        for j, k in enumerate((q, over)):
            send(h0.at[s, k, 1, :, 0:hcols], hx.at[s, k], hx_sem.at[j * n + s], across)

    def cross_g(s):
        send(g0.at[s, :, 1, :, 0:gcols], gx.at[s], gx_sem.at[s], across)

    start_g(0)
    first_g()
    send(gys, gyr, y_sem.at[0], across)

    @pl.when(inner)
    def _():
        signal(two_sem, outward)
        signal(two_sem, inward)

    pick_rows(pick_h, hidden, h0s, hys)
    start_h(0, mate)
    start_h(0, mirror, inner)
    own_fan(0)
    send(hys, hyr, y_sem.at[1], across)
    plane_g(0)
    pl.semaphore_wait(two_sem, 1)
    pl.when(inner)(lambda: signal(three_sem, outward))
    start_h(0, jump)
    fan_h(0, mate)
    pl.when(jnp.logical_not(inner))(lambda: pl.semaphore_wait(three_sem, 1))
    start_h(0, mirror, jnp.logical_not(inner), True)
    forward_near(0)
    landed(gyr, y_sem.at[0])
    for b in (0, 1):
        gbs[b] = gbs[b] + gyr[:, :, b * side : (b + 1) * side]
        start_g(1 + b)
    fan_h(0, jump)
    fan_h(0, mirror)
    for s in (z,) + others:
        relay_h(0, s)
    landed(hyr, y_sem.at[1])
    hbs[...] = hbs[...] + hyr[...]
    for s in others:
        start_h(1, s)
    own_fan(1)
    own_h(0).wait()
    own_g(0).wait()
    cross_h(z)
    cross_g(z)
    finish_g(0, mate)
    cross_h(mate)
    cross_g(mate)
    forward_far(0)
    plane_g(1)
    for s in (jump, mirror):
        cross_h(s)
        finish_g(0, s)
        cross_g(s)
    fan_h(1, mate)
    forward_near(1)
    plane_g(2)
    fan_h(1, jump)
    fan_h(1, mirror)
    forward_far(1)
    kept = keep[0]
    for i in range(1, n * n):
        kept = kept + keep[i]
    factor_out[...] = jnp.float32(n * n) / jnp.maximum(
        jnp.full((half, LANES), kept, jnp.int32).astype(jnp.float32), 1.0
    )
    for s in (z,) + others:
        relay_h(1, s)
    landed(h0.at[0:2], fin_sem.at[0])
    for s in range(n):
        rows_at = slice(s * n * SUB, (s + 1) * n * SUB)
        flat = h0[s, :, :, :, 0:hcols].astype(jnp.float32).reshape(n * SUB, hcols)
        hall[rows_at] = flat.astype(jnp.bfloat16)
        flag = h0[s, :, 1, :, hcols : hcols + LANES].astype(jnp.float32)
        for c in range(gcols // LANES):
            at = c * LANES
            sure = g0[s, :, 0, :, at : at + LANES].astype(jnp.float32)
            spare = g0[s, :, 1, :, at : at + LANES].astype(jnp.float32) * flag
            part = jnp.stack([sure, spare], axis=1).reshape(n * SUB, LANES)
            sides[at // side][rows_at, at % side : at % side + LANES] = part.astype(jnp.bfloat16)
    for s in (z,) + others:
        for j, k in enumerate((q, over)):
            view = hx.at[s, k]
            landed(view, hx_sem.at[j * n + s])
            send(view, view, fin_sem.at[2], beside)
    for s in range(n):
        landed(gx.at[s], gx_sem.at[s])
        rows_at = slice(n_both + s * n * half, n_both + (s + 1) * n * half)
        flag = h0[s, :, 1, :, hcols : hcols + LANES].astype(jnp.float32)
        for c in range(gcols // LANES):
            at = c * LANES
            part = gx[s, :, :, at : at + LANES].astype(jnp.float32) * flag
            part = part.reshape(n * half, LANES).astype(jnp.bfloat16)
            sides[at // side][rows_at, at % side : at % side + LANES] = part
    own_h(1).wait()
    landed(hall.at[pl.ds(n_first, 2 * n * SUB)], fin_sem.at[1])
    landed(hx.at[0:2], fin_sem.at[2])
    for s in range(n):
        rows_at = slice(n_both + s * n * half, n_both + (s + 1) * n * half)
        flat = hx[s].astype(jnp.float32).reshape(n * half, hcols)
        hall[rows_at] = flat.astype(jnp.bfloat16)
    for s in others:
        finish_g(1, s)
    step = made.shape[1]

    def leave(i, blocks, spun):
        at = pl.ds(pl.multiple_of(i * step, step), step)
        for b, block in enumerate(blocks):
            done[at, b * LANES : (b + 1) * LANES] = block
            tops[b, :, at] = spun[b : b + 1]

    forward_near(2)
    forward_far(2)
    block_grads(hall, g_left, factor_out[0:1], made, leave)
    for s in others:
        finish_g(2, s)
    landed(h0.at[0, 0:3], send_sem.at[2])
    landed(h0.at[0:2], send_sem.at[3])
    landed(h0.at[0], send_sem.at[4])
    landed(done.at[pl.ds(0, sent[0] // (2 * side))], send_sem.at[0])

    @pl.when(inner)
    def _():
        landed(done.at[pl.ds(0, sent[1] // (2 * side))], send_sem.at[1])


def grad_pairs(hidden, out_grad, counts, route_index, keep, capacity):
    replicas = lax.axis_size("dp")
    n = math.isqrt(replicas)
    hcols, gcols = hidden.shape[1] // n, out_grad.shape[1] // n
    half, side = SUB // 2, gcols // 2
    depth = 2 * n * n * SUB + n * n * half
    step = min(hcols, 512)
    kind = jnp.bfloat16
    vmem = pl.BlockSpec(memory_space=pltpu.VMEM)
    made = pl.pallas_call(
        functools.partial(spread_kernel, n, hidden.shape[0] - capacity),
        out_shape=[
            jax.ShapeDtypeStruct((depth, hcols), kind),
            jax.ShapeDtypeStruct((depth, side), kind),
            jax.ShapeDtypeStruct((depth, side), kind),
            jax.ShapeDtypeStruct((hcols, side), jnp.float32),
            jax.ShapeDtypeStruct((side // LANES, 1, hcols), jnp.float32),
            jax.ShapeDtypeStruct((half, LANES), jnp.float32),
        ],
        in_specs=[pl.BlockSpec(memory_space=pltpu.HBM)] * 5,
        out_specs=[vmem] * 6,
        scratch_shapes=[
            pltpu.SMEM(counts.shape, counts.dtype),
            pltpu.SMEM(keep.shape, keep.dtype),
            pltpu.VMEM(route_index.shape, route_index.dtype),
            pltpu.VMEM(hidden.shape, kind),
            pltpu.VMEM(out_grad.shape, kind),
            pltpu.VMEM((n, n, 2, half, hcols + LANES), kind),
            pltpu.VMEM((n, n, 2, half, gcols), kind),
            pltpu.VMEM((n, n, half, hcols), kind),
            pltpu.VMEM((n, n, half, gcols), kind),
            pltpu.VMEM((n, 2, half, hcols + LANES), kind),
            pltpu.VMEM((n, 2, half, gcols), kind),
            pltpu.VMEM((n, SUB, hcols), kind),
            pltpu.VMEM((2, n, SUB, side), kind),
            pltpu.VMEM((n, SUB, hcols), kind),
            pltpu.VMEM((n, SUB, gcols), kind),
            pltpu.VMEM((n, SUB, hcols), kind),
            pltpu.VMEM((n, SUB, gcols), kind),
            pltpu.VMEM((2, step, side), jnp.float32),
            pltpu.SemaphoreType.DMA((3 + 2 * n,)),
            pltpu.SemaphoreType.DMA((5,)),
            pltpu.SemaphoreType.DMA((4 * n,)),
            pltpu.SemaphoreType.DMA((3 * n * n,)),
            pltpu.SemaphoreType.DMA((2 * n,)),
            pltpu.SemaphoreType.DMA((n,)),
            pltpu.SemaphoreType.DMA((2,)),
            pltpu.SemaphoreType.DMA((3,)),
            pltpu.SemaphoreType.DMA((5,)),
            pltpu.SemaphoreType.REGULAR,
            pltpu.SemaphoreType.REGULAR,
        ],
        compiler_params=pltpu.CompilerParams(
            collective_id=0, has_side_effects=True, vmem_limit_bytes=36 << 20
        ),
        name="spread",
    )(*[pltpu.with_memory_space_constraint(x, pltpu.HBM) for x in (counts, keep, route_index, hidden, out_grad)])
    hall, _, g_right, done, tops, factor = made
    return pl.pallas_call(
        functools.partial(last_kernel, step),
        out_shape=[
            jax.ShapeDtypeStruct((hcols, gcols), jnp.float32),
            jax.ShapeDtypeStruct((gcols // LANES, 1, hcols), jnp.float32),
        ],
        in_specs=[vmem] * 5,
        out_specs=[pl.BlockSpec(memory_space=pltpu.HBM)] * 2,
        scratch_shapes=[
            pltpu.VMEM((2, step, side), jnp.float32),
            pltpu.VMEM((hcols, side), jnp.float32),
            pltpu.VMEM((side // LANES, 1, hcols), jnp.float32),
            pltpu.SemaphoreType.DMA((hcols // step,)),
            pltpu.SemaphoreType.DMA((3,)),
        ],
        compiler_params=pltpu.CompilerParams(vmem_limit_bytes=20 << 20),
        name="last_side",
    )(hall, g_right, done, tops, factor)


def last_kernel(step, hall, g_right, done, tops, factor, out, scales, made, left, marks, sems, done_sem):
    rows, side = done.shape
    first = pltpu.make_async_copy(done, out.at[:, 0:side], done_sem.at[0])
    first.start()
    count = tops.shape[0]
    ready = pltpu.make_async_copy(tops, scales.at[0:count], done_sem.at[1])
    ready.start()
    fresh = pltpu.make_async_copy(marks, scales.at[count : 2 * count], done_sem.at[2])

    def away(i):
        at = pl.ds(pl.multiple_of(i * step, step), step)
        return pltpu.make_async_copy(left.at[at], out.at[at, side : 2 * side], sems.at[i])

    def leave(i, blocks, spun):
        at = pl.ds(pl.multiple_of(i * step, step), step)
        for b, block in enumerate(blocks):
            left[at, b * LANES : (b + 1) * LANES] = block
            marks[b, :, at] = spun[b : b + 1]
        away(i).start()

    block_grads(hall, g_right, factor[0:1], made, leave)
    fresh.start()
    for i in range(rows // step):
        away(i).wait()
    first.wait()
    ready.wait()
    fresh.wait()


def tile_kernel(pairs, keep, *refs):
    out, scales = refs[2 * pairs :]
    replicas = keep.shape[0]
    kept = keep[0]
    for i in range(1, replicas):
        kept = kept + keep[i]
    factor = jnp.float32(replicas) / jnp.maximum(
        jnp.full((1, LANES), kept, jnp.int32).astype(jnp.float32), 1.0
    )
    total = None
    for i in range(pairs):
        term = lax.dot_general(
            refs[2 * i][...],
            refs[2 * i + 1][...],
            (((0,), (0,)), ((), ())),
            preferred_element_type=jnp.float32,
        )
        total = term if total is None else total + term
    tops = []
    for b in range(out.shape[1] // LANES):
        block = total[:, b * LANES : (b + 1) * LANES] * factor
        top = jnp.max(jnp.abs(block), axis=1, keepdims=True)
        out[:, b * LANES : (b + 1) * LANES] = block * (1.0 / (top + 1e-6))
        tops.append(top)
    lane = lax.broadcasted_iota(jnp.int32, (out.shape[0], LANES), 1)
    packed = jnp.zeros((out.shape[0], LANES), jnp.float32)
    for b, top in enumerate(tops):
        packed = jnp.where(lane == b, top, packed)
    spun = packed.T
    for b in range(scales.shape[0]):
        scales[b] = spun[b : b + 1]


def tile_grad(pairs, keep):
    rows, cols = pairs[0][0].shape[1], pairs[0][1].shape[1]
    step = min(rows, 512)
    args, specs = [], []
    for h, g in pairs:
        args += [h, g]
        specs.append(pl.BlockSpec((h.shape[0], step), lambda i: (0, i)))
        specs.append(pl.BlockSpec((g.shape[0], cols), lambda i: (0, 0)))
    return pl.pallas_call(
        functools.partial(tile_kernel, len(pairs)),
        grid=(rows // step,),
        out_shape=[
            jax.ShapeDtypeStruct((rows, cols), jnp.float32),
            jax.ShapeDtypeStruct((cols // LANES, 1, rows), jnp.float32),
        ],
        in_specs=[pl.BlockSpec(memory_space=pltpu.SMEM)] + specs,
        out_specs=[
            pl.BlockSpec((step, cols), lambda i: (i, 0)),
            pl.BlockSpec((cols // LANES, 1, step), lambda i: (0, 0, i)),
        ],
        compiler_params=pltpu.CompilerParams(vmem_limit_bytes=32 << 20),
        name="tile_grad",
    )(keep, *args)


def on_device(hidden, out_grad, counts, route_index, keep):
    experts = lax.axis_size("expert")
    tok_rows = hidden.shape[0]
    capacity = max(tok_rows // 4, tok_rows // experts + 4)
    low = tok_rows - capacity
    paired = (
        experts == 2
        and lax.axis_size("dp") == 16
        and low == SUB - 4
        and capacity - low == SUB // 2
    )
    operands = (hidden, out_grad, counts, route_index, keep, capacity)
    if paired:
        normed, scales = grad_pairs(*operands)
    else:
        normed, scales = tile_grad(gather_general(*operands), keep)
    return (normed[None, None], jnp.transpose(scales[None], (0, 2, 3, 1)))


def solution(mesh):
    placed = (
        P(("dp", "expert"), None),
        P(("dp", "expert"), None),
        P(("dp", "expert"), None),
        P(("dp", "expert"), None),
        P(),
    )
    return jax.shard_map(
        on_device,
        mesh=mesh,
        in_specs=placed,
        out_specs=(P("expert", "dp", None, None), P("expert", "dp", None, None)),
        check_vma=False,
    )
```

```python
import functools
import math

import jax
import jax.numpy as jnp
from jax import lax
from jax.experimental import pallas as pl
from jax.experimental.pallas import tpu as pltpu
from jax.sharding import PartitionSpec as P

MESH = pl.DeviceIdType.MESH
LANES = 128
SUB = 16


def swapped(block, axis, bit):
    count = lax.axis_size(axis)
    route = []
    for low in range(count):
        high = low | 1 << bit
        if high != low and high < count:
            route += [(low, high), (high, low)]
    return lax.ppermute(block, axis, route)


def build_slots(rows_dev, counts_dev, perm_dev, capacity):
    ids = jnp.arange(counts_dev.shape[0], dtype=jnp.int32)
    before = ids[None, :] < ids[:, None]
    offsets = jnp.sum(jnp.where(before, counts_dev[None, :], 0), axis=1)
    slots = jnp.arange(capacity, dtype=jnp.int32)
    position = offsets[:, None] + slots[None, :]
    position = jnp.minimum(position, rows_dev.shape[0] - 1)
    live = slots[None, :] < counts_dev[:, None]
    local = perm_dev[position]
    picked = rows_dev[local]
    return jnp.where(live[:, :, None], picked, jnp.zeros_like(picked))


def join_pair(mine, partner, replica, bit):
    lower = replica >> bit & 1 == 0
    first = jnp.concatenate([mine, partner], axis=1)
    second = jnp.concatenate([partner, mine], axis=1)
    return jnp.where(lower, first, second)


def gather_general(hidden, out_grad, counts, route_index, keep, capacity):
    experts = lax.axis_size("expert")
    replicas = lax.axis_size("dp")
    side = math.isqrt(replicas)
    levels = side.bit_length() - 1
    replica = lax.axis_index("dp")
    hidden_units = hidden.shape[1]
    width = out_grad.shape[1]
    grad_rows = jnp.where(keep[replica] > 0, out_grad, jnp.zeros_like(out_grad))
    send_h = build_slots(hidden, counts[0], route_index[0], capacity)
    send_g = build_slots(grad_rows, counts[0], route_index[0], capacity)
    recv_h = lax.all_to_all(send_h, "expert", split_axis=0, concat_axis=0, tiled=True)
    recv_g = lax.all_to_all(send_g, "expert", split_axis=0, concat_axis=0, tiled=True)
    slot_count = experts * capacity
    tile_rows = hidden_units // side
    tile_cols = width // side
    sub_rows = slot_count // side
    piece_h = (
        recv_h.reshape(side, sub_rows, side, tile_rows)
        .transpose(2, 0, 1, 3)
        .reshape(replicas, sub_rows, tile_rows)
    )
    piece_g = (
        recv_g.reshape(side, sub_rows, side, tile_cols)
        .transpose(0, 2, 1, 3)
        .reshape(replicas, sub_rows, tile_cols)
    )
    all_h = lax.all_to_all(piece_h, "dp", split_axis=0, concat_axis=0, tiled=True)
    all_g = lax.all_to_all(piece_g, "dp", split_axis=0, concat_axis=0, tiled=True)
    for bit in range(levels):
        all_h = join_pair(all_h, swapped(all_h, "dp", bit), replica, bit)
    for bit in range(levels, 2 * levels):
        all_g = join_pair(all_g, swapped(all_g, "dp", bit), replica, bit)
    return [(all_h.reshape(-1, tile_rows), all_g.reshape(-1, tile_cols))]


def block_grads(h_ref, g_ref, factor, made, leave):
    step = made.shape[1]
    steps = h_ref.shape[1] // step

    def product(i, slot):
        made[slot] = lax.dot_general(
            h_ref[:, pl.ds(pl.multiple_of(i * step, step), step)],
            g_ref[...],
            (((0,), (0,)), ((), ())),
            preferred_element_type=jnp.float32,
        )

    def normalise(i, slot):
        lane = lax.broadcasted_iota(jnp.int32, (step, LANES), 1)
        packed = jnp.zeros((step, LANES), jnp.float32)
        blocks = []
        for b in range(g_ref.shape[1] // LANES):
            block = made[slot, :, b * LANES : (b + 1) * LANES] * factor
            top = jnp.max(jnp.abs(block), axis=1, keepdims=True)
            blocks.append(block * (1.0 / (top + 1e-6)))
            packed = jnp.where(lane == b, top, packed)
        leave(i, blocks, packed.T)

    product(0, 0)

    @pl.loop(0, steps // 2)
    def _(j):
        product(2 * j + 1, 1)
        normalise(2 * j, 0)
        product(jnp.minimum(2 * j + 2, steps - 1), 0)
        normalise(2 * j + 1, 1)


def spread_kernel(
    n, low, counts_in, keep_in, route_in, hidden_in, grad_in,
    hall, g_right, done, tops, factor_out,
    g_left, counts, keep, route, hidden, grad, h0, g0, hx, gx, h0s, g0s, hbs, gbs, hys, gys, hyr, gyr,
    made, in_sem, send_sem, h_sem, g_sem, hx_sem, gx_sem, y_sem, fin_sem, own_sem, two_sem, three_sem,
):
    here = lax.axis_index("dp")
    y = lax.axis_index("expert")
    z, q = here // n, here % n
    twin = q + 1 - 2 * (q % 2)
    over = (q + n // 2) % n
    far = (twin + n // 2) % n
    mate = z + 1 - 2 * (z % 2)
    jump = (z + 2) % n
    mirror = n - 1 - z
    others = (mate, jump, mirror)
    inner = jnp.logical_and(z >= 1, z + 1 < n)
    half = SUB // 2
    n_first = n * n * SUB
    n_both = 2 * n_first
    hcols, gcols = hall.shape[1], gx.shape[3]
    side = gcols // 2

    across = (here, 1 - y)
    beside = (z * n + twin, y)
    outward = (mate * n + q, y)
    inward = (mirror * n + q, y)

    def signal(sem, peer):
        pl.semaphore_signal(sem, inc=1, device_id=peer, device_id_type=MESH)

    barrier = pltpu.get_barrier_semaphore()
    for peer in (across, (z * n + over, y), (z * n + far, y), beside, outward):
        signal(barrier, peer)
    pl.when(inner)(lambda: signal(barrier, inward))

    moves = []
    for src, dst in ((counts_in, counts), (keep_in, keep), (route_in, route)):
        moves.append(pltpu.make_async_copy(src, dst, in_sem.at[len(moves)]))
    for src, dst in ((grad_in, grad), (hidden_in, hidden)):
        cols = src.shape[1] // n
        for part in range(n):
            cut = (slice(None), pl.ds(part * cols, cols))
            moves.append(pltpu.make_async_copy(src.at[cut], dst.at[cut], in_sem.at[len(moves)]))
    for move in moves:
        move.start()

    for move in moves[:3]:
        move.wait()
    due = moves[3:]
    rows = hidden.shape[0]
    total = 3 * SUB
    row = lax.broadcasted_iota(jnp.int32, (total, rows), 0)
    pos = lax.broadcasted_iota(jnp.int32, (total, rows), 1)
    first, second = counts[0, 0], counts[0, 1]
    hot = jnp.where(first > second, 0, 1)
    in_spare = jnp.logical_and(row >= half, row < SUB)
    in_send = row >= 2 * SUB
    expert = jnp.where(in_spare, hot, jnp.where(in_send, 1 - y, y))
    slot = jnp.where(row < half, row, row - half + low)
    slot = jnp.where(row >= SUB, row - SUB - low + half, slot)
    slot = jnp.where(in_send, row - 2 * SUB, slot)
    low_slot = jnp.where(in_send, 0, jnp.where(row < SUB, 0, half))
    high_slot = jnp.where(in_send, low, jnp.where(row < SUB, rows, low))
    valid = jnp.logical_and(slot >= low_slot, slot < high_slot)
    start = jnp.where(expert == 0, 0, first)
    count = jnp.where(expert == 0, first, second)
    take = jnp.logical_and(valid, jnp.logical_and(slot < count, pos == start + slot))
    take = jnp.where(take, 1.0, 0.0).astype(jnp.bfloat16)
    local = lax.broadcasted_iota(jnp.int32, (rows, rows), 0)
    perm = jnp.where(local == route[...], 1.0, 0.0).astype(jnp.bfloat16)
    pick = lax.dot_general(
        take, perm, (((1,), (1,)), ((), ())), preferred_element_type=jnp.float32
    )
    pick_h = pick.astype(jnp.bfloat16)
    pick_g = jnp.where(keep[here] > 0, pick, 0.0).astype(jnp.bfloat16)

    def pick_rows(pick_x, src, x0s, xys):
        cols = xys.shape[2]
        for part in range(n):
            due.pop(0).wait()
            got = jnp.dot(
                pick_x,
                src[:, part * cols : (part + 1) * cols],
                preferred_element_type=jnp.float32,
            )
            x0s[part, 0, :, 0:cols] = got[:half].astype(jnp.bfloat16)
            x0s[part, 1, :, 0:cols] = got[half:SUB].astype(jnp.bfloat16)
            xys[part] = got[2 * SUB :].astype(jnp.bfloat16)
            rest = got[SUB : 2 * SUB].astype(jnp.bfloat16)
            if x0s is h0s:
                hbs[part] = rest
            else:
                gbs[0, part] = rest[:, :side]
                gbs[1, part] = rest[:, side:]

    mine = jnp.ones((half, LANES), jnp.float32) * jnp.where(hot == y, 1.0, 0.0)
    for part in range(n):
        h0s[part, 0, :, hcols : hcols + LANES] = jnp.ones((half, LANES), jnp.bfloat16)
        h0s[part, 1, :, hcols : hcols + LANES] = mine.astype(jnp.bfloat16)
    pick_rows(pick_g, grad, g0s, gys)
    enter = 5 + jnp.minimum(z, 1) * jnp.minimum(n - 1 - z, 1)
    pl.semaphore_wait(barrier, enter)

    sent = [0] * 5

    def send(src, dst, sem, peer, when=None, group=0, again=False):
        if not again:
            sent[group] += math.prod(src.shape)
        copy = pltpu.make_async_remote_copy(
            src_ref=src,
            dst_ref=dst,
            send_sem=send_sem.at[group],
            recv_sem=sem,
            device_id=peer,
            device_id_type=MESH,
        )
        if when is None:
            copy.start()
        else:
            pl.when(when)(copy.start)

    def landed(view, sem):
        pltpu.make_async_copy(view, view, sem).wait()

    sides = (g_left, g_right)

    def h_view(b, s, k):
        if b == 0:
            return h0.at[s, k]
        return hall.at[pl.ds(pl.multiple_of(n_first + (s * n + k) * SUB, SUB), SUB)]

    def g_view(b, s, k, chunks=1):
        if b == 0:
            return g0.at[s, k]
        at = pl.multiple_of(n_first + (s * n + k) * SUB, SUB)
        return sides[b - 1].at[pl.ds(at, chunks * SUB)]

    h_own = lambda b, k: (h0s, hbs)[b].at[k]
    g_own = lambda b, k: g0s.at[k] if b == 0 else gbs.at[b - 1, k]
    h_at = lambda b, s: h_sem.at[2 * n * b + s]
    h_over = lambda b, s: h_sem.at[2 * n * b + n + s]
    g_at = lambda b, s, k: g_sem.at[(b * n + s) * n + k]
    chunks = lambda b: [(k, 1) for k in (q, twin, over, far)] if b == 0 else [(q - q % 2, 2), (over - over % 2, 2)]

    def own_h(b):
        return pltpu.make_async_copy(h_own(b, z), h_view(b, z, q), own_sem.at[b])

    def own_g(b):
        return pltpu.make_async_copy(g_own(b, q), g_view(b, z, q), own_sem.at[2 + b])

    def start_g(b):
        for to in (over, far, twin):
            send(g_own(b, to), g_view(b, z, q), g_at(b, z, q), (z * n + to, y))
        own_g(b).start()

    def both_ways(view, sem):
        send(view, view, sem, outward)
        send(view, view, sem, inward, inner, 1)

    def first_g():
        send(g_own(0, q), g_view(0, z, q), g_at(0, z, q), outward)
        send(g_own(0, q), g_view(0, z, q), g_at(0, z, q), inward, inner, 1)

    def plane_g(b):
        if b == 0:
            for k in (twin, over, far):
                landed(g_view(b, z, k), g_at(b, z, k))
                both_ways(g_view(b, z, k), g_at(b, z, k))
            return
        own_g(b).wait()
        for pair in ((twin,), (over, far)):
            for k in pair:
                landed(g_view(b, z, k), g_at(b, z, k))
            k = pair[0] - pair[0] % 2
            both_ways(g_view(b, z, k, 2), g_at(b, z, k))

    def start_h(b, s, when=None, again=False):
        to = (s * n + q, y)
        send(h_own(b, s), h_view(b, z, q), h_at(b, z), to, when, 0 if b else 2, again)

    def own_fan(b):
        group = 0 if b else 3
        send(h_own(b, z), h_view(b, z, q), h_over(b, z), (z * n + over, y), None, group)
        send(h_own(b, z), h_view(b, z, q), fin_sem.at[b], beside, None, group)
        own_h(b).start()

    def forward_g(b, s, peer):
        for k, count in chunks(b):
            view, sem = g_view(b, s, k, count), g_at(b, s, k)
            pl.when(inner)(functools.partial(landed, view, sem))
            send(view, view, sem, peer, inner, 1)

    def forward_near(b):
        forward_g(b, mate, inward)
        forward_g(b, mirror, outward)

    def forward_far(b):
        forward_g(b, jump, outward)

    def finish_g(b, s):
        for k, count in chunks(b):
            pl.when(jnp.logical_not(inner))(
                functools.partial(landed, g_view(b, s, k, count), g_at(b, s, k))
            )

    def fan_h(b, s):
        view, group = h_view(b, s, q), 0 if b else 3
        landed(view, h_at(b, s))
        send(view, view, h_over(b, s), (z * n + over, y), None, group)
        send(view, view, fin_sem.at[b], beside, None, group)

    def relay_h(b, s):
        view = h_view(b, s, over)
        landed(view, h_over(b, s))
        send(view, view, fin_sem.at[b], beside, None, 0 if b else 4)

    def cross_h(s):
        for j, k in enumerate((q, over)):
            send(h0.at[s, k, 1, :, 0:hcols], hx.at[s, k], hx_sem.at[j * n + s], across)

    def cross_g(s):
        send(g0.at[s, :, 1, :, 0:gcols], gx.at[s], gx_sem.at[s], across)

    start_g(0)
    first_g()
    send(gys, gyr, y_sem.at[0], across)

    @pl.when(inner)
    def _():
        signal(two_sem, outward)
        signal(two_sem, inward)

    pick_rows(pick_h, hidden, h0s, hys)
    start_h(0, mate)
    start_h(0, mirror, inner)
    own_fan(0)
    send(hys, hyr, y_sem.at[1], across)
    plane_g(0)
    pl.semaphore_wait(two_sem, 1)
    pl.when(inner)(lambda: signal(three_sem, outward))
    start_h(0, jump)
    fan_h(0, mate)
    pl.when(jnp.logical_not(inner))(lambda: pl.semaphore_wait(three_sem, 1))
    start_h(0, mirror, jnp.logical_not(inner), True)
    forward_near(0)
    landed(gyr, y_sem.at[0])
    for b in (0, 1):
        gbs[b] = gbs[b] + gyr[:, :, b * side : (b + 1) * side]
        start_g(1 + b)
    fan_h(0, jump)
    fan_h(0, mirror)
    for s in (z,) + others:
        relay_h(0, s)
    landed(hyr, y_sem.at[1])
    hbs[...] = hbs[...] + hyr[...]
    for s in others:
        start_h(1, s)
    own_fan(1)
    own_h(0).wait()
    own_g(0).wait()
    cross_h(z)
    cross_g(z)
    finish_g(0, mate)
    cross_h(mate)
    cross_g(mate)
    forward_far(0)
    plane_g(1)
    for s in (jump, mirror):
        cross_h(s)
        finish_g(0, s)
        cross_g(s)
    fan_h(1, mate)
    forward_near(1)
    plane_g(2)
    fan_h(1, jump)
    fan_h(1, mirror)
    forward_far(1)
    kept = keep[0]
    for i in range(1, n * n):
        kept = kept + keep[i]
    factor_out[...] = jnp.float32(n * n) / jnp.maximum(
        jnp.full((half, LANES), kept, jnp.int32).astype(jnp.float32), 1.0
    )
    for s in (z,) + others:
        relay_h(1, s)
    landed(h0.at[0:2], fin_sem.at[0])
    for s in range(n):
        rows_at = slice(s * n * SUB, (s + 1) * n * SUB)
        flat = h0[s, :, :, :, 0:hcols].astype(jnp.float32).reshape(n * SUB, hcols)
        hall[rows_at] = flat.astype(jnp.bfloat16)
        flag = h0[s, :, 1, :, hcols : hcols + LANES].astype(jnp.float32)
        for c in range(gcols // LANES):
            at = c * LANES
            sure = g0[s, :, 0, :, at : at + LANES].astype(jnp.float32)
            spare = g0[s, :, 1, :, at : at + LANES].astype(jnp.float32) * flag
            part = jnp.stack([sure, spare], axis=1).reshape(n * SUB, LANES)
            sides[at // side][rows_at, at % side : at % side + LANES] = part.astype(jnp.bfloat16)
    for s in (z,) + others:
        for j, k in enumerate((q, over)):
            view = hx.at[s, k]
            landed(view, hx_sem.at[j * n + s])
            send(view, view, fin_sem.at[2], beside)
    for s in range(n):
        landed(gx.at[s], gx_sem.at[s])
        rows_at = slice(n_both + s * n * half, n_both + (s + 1) * n * half)
        flag = h0[s, :, 1, :, hcols : hcols + LANES].astype(jnp.float32)
        for c in range(gcols // LANES):
            at = c * LANES
            part = gx[s, :, :, at : at + LANES].astype(jnp.float32) * flag
            part = part.reshape(n * half, LANES).astype(jnp.bfloat16)
            sides[at // side][rows_at, at % side : at % side + LANES] = part
    own_h(1).wait()
    landed(hall.at[pl.ds(n_first, 2 * n * SUB)], fin_sem.at[1])
    landed(hx.at[0:2], fin_sem.at[2])
    for s in range(n):
        rows_at = slice(n_both + s * n * half, n_both + (s + 1) * n * half)
        flat = hx[s].astype(jnp.float32).reshape(n * half, hcols)
        hall[rows_at] = flat.astype(jnp.bfloat16)
    for s in others:
        finish_g(1, s)
    step = made.shape[1]

    def leave(i, blocks, spun):
        at = pl.ds(pl.multiple_of(i * step, step), step)
        for b, block in enumerate(blocks):
            done[at, b * LANES : (b + 1) * LANES] = block
            tops[b, :, at] = spun[b : b + 1]

    forward_near(2)
    forward_far(2)
    block_grads(hall, g_left, factor_out[0:1], made, leave)
    for s in others:
        finish_g(2, s)
    landed(h0.at[0, 0:3], send_sem.at[2])
    landed(h0.at[0:2], send_sem.at[3])
    landed(h0.at[0], send_sem.at[4])
    landed(done.at[pl.ds(0, sent[0] // (2 * side))], send_sem.at[0])

    @pl.when(inner)
    def _():
        landed(done.at[pl.ds(0, sent[1] // (2 * side))], send_sem.at[1])


def grad_pairs(hidden, out_grad, counts, route_index, keep, capacity):
    replicas = lax.axis_size("dp")
    n = math.isqrt(replicas)
    hcols, gcols = hidden.shape[1] // n, out_grad.shape[1] // n
    half, side = SUB // 2, gcols // 2
    depth = 2 * n * n * SUB + n * n * half
    step = min(hcols, 512)
    kind = jnp.bfloat16
    vmem = pl.BlockSpec(memory_space=pltpu.VMEM)
    made = pl.pallas_call(
        functools.partial(spread_kernel, n, hidden.shape[0] - capacity),
        out_shape=[
            jax.ShapeDtypeStruct((depth, hcols), kind),
            jax.ShapeDtypeStruct((depth, side), kind),
            jax.ShapeDtypeStruct((hcols, side), jnp.float32),
            jax.ShapeDtypeStruct((side // LANES, 1, hcols), jnp.float32),
            jax.ShapeDtypeStruct((half, LANES), jnp.float32),
        ],
        in_specs=[pl.BlockSpec(memory_space=pltpu.HBM)] * 5,
        out_specs=[vmem] * 5,
        scratch_shapes=[
            pltpu.VMEM((depth, side), kind),
            pltpu.SMEM(counts.shape, counts.dtype),
            pltpu.SMEM(keep.shape, keep.dtype),
            pltpu.VMEM(route_index.shape, route_index.dtype),
            pltpu.VMEM(hidden.shape, kind),
            pltpu.VMEM(out_grad.shape, kind),
            pltpu.VMEM((n, n, 2, half, hcols + LANES), kind),
            pltpu.VMEM((n, n, 2, half, gcols), kind),
            pltpu.VMEM((n, n, half, hcols), kind),
            pltpu.VMEM((n, n, half, gcols), kind),
            pltpu.VMEM((n, 2, half, hcols + LANES), kind),
            pltpu.VMEM((n, 2, half, gcols), kind),
            pltpu.VMEM((n, SUB, hcols), kind),
            pltpu.VMEM((2, n, SUB, side), kind),
            pltpu.VMEM((n, SUB, hcols), kind),
            pltpu.VMEM((n, SUB, gcols), kind),
            pltpu.VMEM((n, SUB, hcols), kind),
            pltpu.VMEM((n, SUB, gcols), kind),
            pltpu.VMEM((2, step, side), jnp.float32),
            pltpu.SemaphoreType.DMA((3 + 2 * n,)),
            pltpu.SemaphoreType.DMA((5,)),
            pltpu.SemaphoreType.DMA((4 * n,)),
            pltpu.SemaphoreType.DMA((3 * n * n,)),
            pltpu.SemaphoreType.DMA((2 * n,)),
            pltpu.SemaphoreType.DMA((n,)),
            pltpu.SemaphoreType.DMA((2,)),
            pltpu.SemaphoreType.DMA((3,)),
            pltpu.SemaphoreType.DMA((5,)),
            pltpu.SemaphoreType.REGULAR,
            pltpu.SemaphoreType.REGULAR,
        ],
        compiler_params=pltpu.CompilerParams(
            collective_id=0, has_side_effects=True, vmem_limit_bytes=36 << 20
        ),
        name="spread",
    )(*[pltpu.with_memory_space_constraint(x, pltpu.HBM) for x in (counts, keep, route_index, hidden, out_grad)])
    hall, g_right, done, tops, factor = made
    return pl.pallas_call(
        functools.partial(last_kernel, step),
        out_shape=[
            jax.ShapeDtypeStruct((hcols, gcols), jnp.float32),
            jax.ShapeDtypeStruct((gcols // LANES, 1, hcols), jnp.float32),
        ],
        in_specs=[vmem] * 5,
        out_specs=[pl.BlockSpec(memory_space=pltpu.HBM)] * 2,
        scratch_shapes=[
            pltpu.VMEM((2, step, side), jnp.float32),
            pltpu.VMEM((hcols, side), jnp.float32),
            pltpu.VMEM((side // LANES, 1, hcols), jnp.float32),
            pltpu.SemaphoreType.DMA((hcols // step,)),
            pltpu.SemaphoreType.DMA((3,)),
        ],
        compiler_params=pltpu.CompilerParams(vmem_limit_bytes=20 << 20),
        name="last_side",
    )(hall, g_right, done, tops, factor)


def last_kernel(step, hall, g_right, done, tops, factor, out, scales, made, left, marks, sems, done_sem):
    rows, side = done.shape
    first = pltpu.make_async_copy(done, out.at[:, 0:side], done_sem.at[0])
    first.start()
    count = tops.shape[0]
    ready = pltpu.make_async_copy(tops, scales.at[0:count], done_sem.at[1])
    ready.start()
    fresh = pltpu.make_async_copy(marks, scales.at[count : 2 * count], done_sem.at[2])

    def away(i):
        at = pl.ds(pl.multiple_of(i * step, step), step)
        return pltpu.make_async_copy(left.at[at], out.at[at, side : 2 * side], sems.at[i])

    def leave(i, blocks, spun):
        at = pl.ds(pl.multiple_of(i * step, step), step)
        for b, block in enumerate(blocks):
            left[at, b * LANES : (b + 1) * LANES] = block
            marks[b, :, at] = spun[b : b + 1]
        away(i).start()

    block_grads(hall, g_right, factor[0:1], made, leave)
    fresh.start()
    for i in range(rows // step):
        away(i).wait()
    first.wait()
    ready.wait()
    fresh.wait()


def tile_kernel(pairs, keep, *refs):
    out, scales = refs[2 * pairs :]
    replicas = keep.shape[0]
    kept = keep[0]
    for i in range(1, replicas):
        kept = kept + keep[i]
    factor = jnp.float32(replicas) / jnp.maximum(
        jnp.full((1, LANES), kept, jnp.int32).astype(jnp.float32), 1.0
    )
    total = None
    for i in range(pairs):
        term = lax.dot_general(
            refs[2 * i][...],
            refs[2 * i + 1][...],
            (((0,), (0,)), ((), ())),
            preferred_element_type=jnp.float32,
        )
        total = term if total is None else total + term
    tops = []
    for b in range(out.shape[1] // LANES):
        block = total[:, b * LANES : (b + 1) * LANES] * factor
        top = jnp.max(jnp.abs(block), axis=1, keepdims=True)
        out[:, b * LANES : (b + 1) * LANES] = block * (1.0 / (top + 1e-6))
        tops.append(top)
    lane = lax.broadcasted_iota(jnp.int32, (out.shape[0], LANES), 1)
    packed = jnp.zeros((out.shape[0], LANES), jnp.float32)
    for b, top in enumerate(tops):
        packed = jnp.where(lane == b, top, packed)
    spun = packed.T
    for b in range(scales.shape[0]):
        scales[b] = spun[b : b + 1]


def tile_grad(pairs, keep):
    rows, cols = pairs[0][0].shape[1], pairs[0][1].shape[1]
    step = min(rows, 512)
    args, specs = [], []
    for h, g in pairs:
        args += [h, g]
        specs.append(pl.BlockSpec((h.shape[0], step), lambda i: (0, i)))
        specs.append(pl.BlockSpec((g.shape[0], cols), lambda i: (0, 0)))
    return pl.pallas_call(
        functools.partial(tile_kernel, len(pairs)),
        grid=(rows // step,),
        out_shape=[
            jax.ShapeDtypeStruct((rows, cols), jnp.float32),
            jax.ShapeDtypeStruct((cols // LANES, 1, rows), jnp.float32),
        ],
        in_specs=[pl.BlockSpec(memory_space=pltpu.SMEM)] + specs,
        out_specs=[
            pl.BlockSpec((step, cols), lambda i: (i, 0)),
            pl.BlockSpec((cols // LANES, 1, step), lambda i: (0, 0, i)),
        ],
        compiler_params=pltpu.CompilerParams(vmem_limit_bytes=32 << 20),
        name="tile_grad",
    )(keep, *args)


def on_device(hidden, out_grad, counts, route_index, keep):
    experts = lax.axis_size("expert")
    tok_rows = hidden.shape[0]
    capacity = max(tok_rows // 4, tok_rows // experts + 4)
    low = tok_rows - capacity
    paired = (
        experts == 2
        and lax.axis_size("dp") == 16
        and low == SUB - 4
        and capacity - low == SUB // 2
    )
    operands = (hidden, out_grad, counts, route_index, keep, capacity)
    if paired:
        normed, scales = grad_pairs(*operands)
    else:
        normed, scales = tile_grad(gather_general(*operands), keep)
    return (normed[None, None], jnp.transpose(scales[None], (0, 2, 3, 1)))


def solution(mesh):
    placed = (
        P(("dp", "expert"), None),
        P(("dp", "expert"), None),
        P(("dp", "expert"), None),
        P(("dp", "expert"), None),
        P(),
    )
    return jax.shard_map(
        on_device,
        mesh=mesh,
        in_specs=placed,
        out_specs=(P("expert", "dp", None, None), P("expert", "dp", None, None)),
        check_vma=False,
    )
```
